32 devices in a mesh: az: 4 (over x, core), rad: 8 (over z, y).
Axes of the slice: x: 2, y: 2, z: 4, core: 2. Of those that a mesh axis runs over, the one named last changes fastest.
Arguments:
- fields: float32 [4, 16, 64, 512], P(None, None, 'rad', 'az'), may hold values from -6 to 6, as said below
- shifts: int32 [16, 64], P(None, 'rad'), may hold values from 0 to 511, as said below
- courant: float32 [16, 64], P(None, 'rad'), may hold values from -0.45 to 0.45
Outputs:
- advanced: float32 [4, 16, 64, 512], P(None, None, 'rad', 'az')
The draws below stay inside these ranges and needn't reach their ends.
Inputs may be any that keep to these rules, and one draw needn't show every extreme that they name: fields 0 and 1 (velocities) lie in the range; fields 2 and 3 (energy, density) lie between 0.5 and 2. `shifts`: any whole shift of a cycle in cells.
All inputs are finite; a program needn't handle non-finite values.
Results may differ from the reference program's by a relative error of at most 0.0003.
Values sent between devices are 32-bit elements; how exact they have to be, the bound alone decides.
A program may use at most 64 MiB of HBM per device.

```python
import math
import jax
import jax.numpy as jnp
from jax import lax

NTH = 16
NPHI = 512
NR = 64


def draw_fields(key, part):
    keys = jax.random.split(jax.random.fold_in(key, 11), 2)
    low = math.log(0.5)
    high = math.log(2.0)
    velocity = jax.random.truncated_normal(keys[0], -6.0, 6.0, (2, NTH, NR, NPHI), jnp.float32)
    positive = jnp.exp(jax.random.uniform(keys[1], (2, NTH, NR, NPHI), jnp.float32, low, high))
    return jnp.concatenate([velocity, positive], axis=0)


def draw_shifts(key, part):
    values = jax.random.randint(jax.random.fold_in(key, 23), (NTH, NR), 0, NPHI, jnp.int32)
    values = values.at[0, 0].set(NPHI - 1)
    return values.at[0, 1].set(0)


def shard_levels(stream_key, dims, shards, least, high):
    loudness = 1.0
    for position, parts in shards:
        heights = jax.random.uniform(jax.random.fold_in(jax.random.fold_in(stream_key, 6), position), (parts,), jnp.float32, least / len(shards), high / len(shards))
        loudness = loudness * jnp.repeat(jnp.exp(heights), dims[position] // parts).reshape((-1,) + (1,) * (len(dims) - 1 - position))
    return loudness


def setup_inputs(seed: int = 0) -> dict:
    seeds = jax.random.split(jax.random.key(seed), 4)
    fields = draw_fields(jax.random.fold_in(seeds[3], 71), 0)
    shifts = draw_shifts(jax.random.fold_in(seeds[3], 71), 0)
    courant = jnp.clip(jax.random.uniform(seeds[2], (NTH, NR), jnp.float32, -0.45, 0.45) * shard_levels(seeds[2], (NTH, NR), ((1, 8),), -0.4, 0.0), -0.45, 0.45)
    return dict(fields=fields, shifts=shifts, courant=courant)


inner_radius = 0.4
adiabatic = 1.4


def minmod(left, right):
    return 0.5 * (jnp.sign(left) + jnp.sign(right)) * jnp.minimum(jnp.abs(left), jnp.abs(right))


def limited(extended, courant_cycle):
    differences = extended[..., 1:] - extended[..., :-1]
    slopes = minmod(differences[..., :-1], differences[..., 1:])
    centers = extended[..., 1:-1]
    flux_plus = courant_cycle * (centers[..., :-1] + 0.5 * (1.0 - courant_cycle) * slopes[..., :-1])
    flux_minus = courant_cycle * (centers[..., 1:] - 0.5 * (1.0 + courant_cycle) * slopes[..., 1:])
    face_flux = jnp.where(courant_cycle >= 0.0, flux_plus, flux_minus)
    return extended[..., 2:-2] - (face_flux[..., 1:] - face_flux[..., :-1])


def center(field):
    return field[..., 1:-1, 1:-1]


def across_az(field):
    return field[..., 1:-1, 2:] - field[..., 1:-1, :-2]


def across_rad(field):
    return field[..., 2:, 1:-1] - field[..., :-2, 1:-1]


def laplace(field, phi_width, rad_step):
    middle = center(field)
    along_az = (field[..., 1:-1, 2:] + field[..., 1:-1, :-2] - 2.0 * middle) / (phi_width * phi_width)
    along_rad = (field[..., 2:, 1:-1] + field[..., :-2, 1:-1] - 2.0 * middle) / (rad_step * rad_step)
    return along_az + along_rad


def stencil(padded, density, radius, phi_count, rad_count):
    phi_step = 2.0 * math.pi / phi_count
    rad_step = 1.0 / rad_count
    spacing = min(rad_step, inner_radius * phi_step)
    time_step = 0.2 * spacing
    viscosity = 0.05 * spacing * spacing / time_step
    radial_vel = padded[0]
    azim_vel = padded[1]
    energy = padded[2]
    pressure = (adiabatic - 1.0) * energy
    phi_width = radius * phi_step
    radial_mid = center(radial_vel)
    azim_mid = center(azim_vel)
    energy_mid = center(energy)
    radial_new = radial_mid + time_step * (-across_rad(pressure) * (0.5 / rad_step) / density
                                           + viscosity * laplace(radial_vel, phi_width, rad_step)
                                           + azim_mid * azim_mid / radius - 1.0 / (radius * radius))
    azim_new = azim_mid + time_step * (-across_az(pressure) * 0.5 / (phi_width * density)
                                       + viscosity * laplace(azim_vel, phi_width, rad_step)
                                       - radial_mid * azim_mid / radius)
    divergence = across_rad(radial_vel) * (0.5 / rad_step) + across_az(azim_vel) * 0.5 / phi_width + radial_mid / radius
    energy_new = energy_mid - time_step * (adiabatic - 1.0) * energy_mid * divergence
    return radial_new, azim_new, energy_new


def reference(fields, shifts, courant):
    radius = (inner_radius + (jnp.arange(NR).astype(jnp.float32) + 0.5) * (1.0 / NR))[:, None]

    def one_slice(inputs):
        slab, cycle_shift, cycle_courant = inputs
        padded = jnp.pad(slab[0:3], ((0, 0), (1, 1), (0, 0)), mode="edge")
        padded = jnp.concatenate([padded[..., -1:], padded, padded[..., :1]], axis=-1)
        radial_new, azim_new, energy_new = stencil(padded, slab[3], radius, NPHI, NR)
        moved = jnp.stack([radial_new, azim_new, energy_new, slab[3]])
        take_index = (jnp.arange(NPHI).astype(jnp.int32)[None, :] - cycle_shift[:, None]) % NPHI
        take_index = jnp.broadcast_to(take_index[None], moved.shape)
        shifted = jnp.take_along_axis(moved, take_index, axis=-1)
        extended = jnp.concatenate([shifted[..., -2:], shifted, shifted[..., :2]], axis=-1)
        return limited(extended, cycle_courant[None, :, None])

    advanced = lax.map(one_slice, (jnp.moveaxis(fields, 1, 0), shifts, courant))
    return jnp.moveaxis(advanced, 0, 1)
```

```python
import functools
import math

import jax
import jax.numpy as jnp
from jax import lax
from jax.experimental import pallas as pl
from jax.experimental.pallas import tpu as pltpu
from jax.sharding import PartitionSpec as P

inner_radius = 0.4
adiabatic = 1.4
MESH = pl.DeviceIdType.MESH
OFFSETS = (-2, -1, 0, 1)
BOUNDS = (0, 4, 9, 13, 15, 16)


def remote(src, dst, send, recv, az, rad):
    return pltpu.make_async_remote_copy(
        src_ref=src,
        dst_ref=dst,
        send_sem=send,
        recv_sem=recv,
        device_id={"az": az, "rad": rad},
        device_id_type=MESH,
    )


def minmod(a, b):
    return jnp.maximum(jnp.minimum(a, b), 0.0) + jnp.minimum(jnp.maximum(a, b), 0.0)


def kernel(n, rn, bounds, fields, shifts_in, courant_in, out, raw, early, G, H, ZS, ZR, FX, SEG, LANE, CA, shifts, courant,
           local_sem, small_sem, sent, edge_sent, edge_got, side_sent, side_got, fix_sent, fix_got, dens_got, dens_mate, got, mate_got):
    _, T, R, L = fields.shape
    X = n // 2
    K = len(bounds) - 1
    fill = bounds[1]
    az = lax.axis_index("az")
    rad = lax.axis_index("rad")
    x, c = az // 2, az % 2
    mate = x * 2 + (1 - c)
    before, after = lax.rem(az + n - 1, n), lax.rem(az + 1, n)

    def column(k, core=None):
        return lax.rem(x + k, X) * 2 + (c if core is None else core)

    def source(k, core):
        return lax.rem(x + X - k, X) * 2 + core

    has_low, has_high = rad > 0, rad < rn - 1
    sends = (has_high, has_low)
    receives = (has_low, has_high)
    toward = (rad + 1, rad - 1)

    barrier = pltpu.get_barrier_semaphore()

    def greet(a, r):
        pl.semaphore_signal(barrier, inc=1, device_id={"az": a, "rad": r}, device_id_type=MESH)

    greet(mate, rad)
    for k in range(1, X):
        greet(column(k), rad)
        greet(column(k, 1 - c), rad)
    for way in range(2):
        @pl.when(sends[way])
        def _():
            greet(az, toward[way])

    small = (
        pltpu.make_async_copy(shifts_in, shifts, small_sem.at[0]),
        pltpu.make_async_copy(courant_in, courant, small_sem.at[1]),
    )
    local = (
        pltpu.make_async_copy(fields.at[0:3], raw, local_sem.at[0]),
        pltpu.make_async_copy(fields.at[3], G.at[az, 3], local_sem.at[1]),
    )
    for copy in small + local:
        copy.start()

    phi_count, rad_count = n * L, rn * R
    phi_step = 2.0 * math.pi / phi_count
    rad_step = 1.0 / rad_count
    spacing = min(rad_step, inner_radius * phi_step)
    dt = 0.2 * spacing
    viscosity = 0.05 * spacing * spacing / dt
    row = lax.broadcasted_iota(jnp.int32, (R, L), 0)
    lane = lax.broadcasted_iota(jnp.int32, (R, L), 1)
    radius = inner_radius + ((rad * R + row).astype(jnp.float32) + 0.5) * (1.0 / rad_count)
    width = radius * phi_step
    inv_r = 1.0 / radius
    inv_w = 1.0 / width
    spread_az = (dt * viscosity) * inv_w * inv_w
    spread_rad = dt * viscosity / (rad_step * rad_step)
    press_rad = dt * (adiabatic - 1.0) * 0.5 / rad_step
    press_az = (dt * (adiabatic - 1.0) * 0.5) * inv_w
    turn = dt * inv_r
    pull = dt * inv_r * inv_r
    heat = dt * (adiabatic - 1.0)
    heat_rad = heat * 0.5 / rad_step
    heat_az = (heat * 0.5) * inv_w
    heat_r = heat * inv_r
    bits = L.bit_length() - 1
    first_lane, last_lane = lane == 0, lane == L - 1
    first_row, last_row = row == 0, row == R - 1

    def turned(value, amount):
        return pltpu.roll(value, amount % L, 1) if amount % L else value

    for copy in small:
        copy.wait()
    for t in range(T):
        moves = jnp.broadcast_to(shifts[:, t : t + 1], (R, L))
        cour = jnp.broadcast_to(courant[:, t : t + 1], (R, L))
        CA[t] = jnp.abs(cour)
        sign = jnp.where(cour >= 0.0, 1, -1)
        for o, offset in enumerate(OFFSETS):
            s = moves - sign * offset
            s = jnp.where(s < 0, s + phi_count, s)
            s = jnp.where(s >= phi_count, s - phi_count, s)
            q = s >> bits
            rest = s & (L - 1)
            seg = az - q - jnp.where(lane + rest >= L, 1, 0)
            SEG[t, o] = jnp.where(seg < 0, seg + n, seg)
            LANE[t, o] = (lane - rest) & (L - 1)

    for copy in local:
        copy.wait()

    for side in range(2):
        for p in range(ZS.shape[1]):
            packed = jnp.zeros((R, L), jnp.float32)
            for i in range(p * L, min(3 * T, (p + 1) * L)):
                packed = jnp.where(lane == i - p * L, turned(raw[i // T, i % T], i - p * L + side), packed)
            ZS[side, p] = packed

    for way in range(2):
        @pl.when(jnp.logical_not(receives[way]))
        def _():
            H[way] = raw[:, :, (R - 1) * way, :]

    def stencil(t, dst, inner):
        vr, vp, en, den = raw[0, t], raw[1, t], raw[2, t], G[az, 3, t]

        def around(f, q):
            i = f * T + t
            left, right = turned(q, 1), turned(q, L - 1)
            low, high = pltpu.roll(q, 1, 0), pltpu.roll(q, R - 1, 0)
            if not inner:
                left = jnp.where(first_lane, turned(ZR[0, i // L], -i), left)
                right = jnp.where(last_lane, turned(ZR[1, i // L], L - 1 - i), right)
                low = jnp.where(first_row, H[0, f, pl.ds(t, 1), :], low)
                high = jnp.where(last_row, H[1, f, pl.ds(t, 1), :], high)
            return left, right, low, high

        vl, vh, vd, vu = around(0, vr)
        pl_, ph, pd, pu = around(1, vp)
        el, eh, ed, eu = around(2, en)
        inv_den = 1.0 / den
        dst[0, t] = vr + (
            spread_az * (vh + vl - 2.0 * vr)
            + spread_rad * (vu + vd - 2.0 * vr)
            + (vp * vp * turn - pull)
            - press_rad * (eu - ed) * inv_den
        )
        dst[1, t] = vp + (
            spread_az * (ph + pl_ - 2.0 * vp)
            + spread_rad * (pu + pd - 2.0 * vp)
            - vr * vp * turn
            - press_az * (eh - el) * inv_den
        )
        dst[2, t] = en - en * (heat_rad * (vu - vd) + heat_az * (ph - pl_) + heat_r * vr)

    for t in range(fill):
        stencil(t, early, True)

    neighbours = has_low.astype(jnp.int32) + has_high.astype(jnp.int32)
    pl.semaphore_wait(barrier, 2 * X - 1 + neighbours)

    def side_copy(side):
        return remote(ZS.at[side], ZR.at[1 - side], side_sent, side_got, after if side else before, rad)

    def edge_copy(way):
        return remote(raw.at[:, :, (R - 1) * (1 - way), :], H.at[way], edge_sent.at[way], edge_got.at[way], az, toward[way])

    def block(seg, j):
        return G.at[seg, 0:3, pl.ds(bounds[j], bounds[j + 1] - bounds[j])]

    for side in range(2):
        side_copy(side).start()
    for way in range(2):
        @pl.when(sends[way])
        def _():
            edge_copy(way).start()
    for k in range(1, X):
        remote(G.at[az, 3], G.at[az, 3], sent, dens_got.at[k - 1], column(k), rad).start()
    for k in range(1, X):
        inside = pl.ds(1, R - 2)
        remote(early.at[:, :, inside], G.at[az, 0:3, pl.ds(0, fill), inside], sent, got.at[0, k - 1], column(k), rad).start()
    remote(G.at[az, 3], G.at[az, 3], sent, dens_mate, mate, rad).start()

    remote(ZR, ZR, side_sent, side_got, mate, rad).wait_recv()
    for way in range(2):
        @pl.when(receives[way])
        def _():
            remote(H.at[way], H.at[way], edge_sent.at[way], edge_got.at[way], az, rad).wait_recv()

    for j in [1, 0] + list(range(2, K)):
        for t in range(bounds[j], bounds[j + 1]):
            stencil(t, G.at[az], False)
        if j == 0:
            for p in range(FX.shape[1]):
                packed = jnp.zeros((R, L), jnp.float32)
                for i in range(p * L, min(6 * fill, (p + 1) * L)):
                    f, t, side = i // (2 * fill), i // 2 % fill, i % 2
                    packed = jnp.where(lane == i - p * L, turned(G[az, f, t], i - p * L + side), packed)
                FX[az, p] = packed
            for k in range(1, X):
                for r in (0, R - 1):
                    line = G.at[az, 0:3, pl.ds(0, fill), r]
                    remote(line, line, sent, got.at[0, k - 1], column(k), rad).start()
                remote(FX.at[az], FX.at[az], fix_sent, fix_got.at[k - 1], column(k), rad).start()
        else:
            for k in range(1, X):
                remote(block(az, j), block(az, j), sent, got.at[j, k - 1], column(k), rad).start()
                if j == K - 1:
                    remote(block(az, j), block(az, j), sent, mate_got.at[j], column(k, 1 - c), rad).start()
        remote(block(az, j), block(az, j), sent, mate_got.at[j], mate, rad).start()

    def step(t):
        amount = CA[t]
        half = 0.5 * (1.0 - amount)
        taken = [[] for _ in range(4)]
        moved = [[G[s, f, t] for f in range(4)] for s in range(n)]
        for o in range(len(OFFSETS)):
            seg, at = SEG[t, o], LANE[t, o]
            chosen = [seg == s for s in range(n - 1)]
            for f in range(4):
                value = moved[n - 1][f]
                for s in range(n - 1):
                    value = jnp.where(chosen[s], moved[s][f], value)
                taken[f].append(jnp.take_along_axis(value, at, axis=1, mode="promise_in_bounds"))
        for f in range(4):
            q0, q1, q2, q3 = taken[f]
            d0, d1, d2 = q1 - q0, q2 - q1, q3 - q2
            enters = q1 + half * minmod(d0, d1)
            leaves = q2 + half * minmod(d1, d2)
            out[f, t] = q2 - amount * (leaves - enters)

    def take(j):
        for k in range(1, X):
            seg = source(k, c)
            copy = remote(block(seg, j), block(seg, j), sent, got.at[j, k - 1], mate, rad)
            copy.wait_recv()
            if j == 0:
                remote(FX.at[seg], FX.at[seg], fix_sent, fix_got.at[k - 1], mate, rad).wait_recv()
                for i in range(3 * fill):
                    f, t = i // fill, i % fill
                    p, at = 2 * i // L, 2 * i % L
                    value = jnp.where(first_lane, turned(FX[seg, p], -at), G[seg, f, t])
                    G[seg, f, t] = jnp.where(last_lane, turned(FX[seg, p], L - 2 - at), value)
            if j < K - 1:
                remote(block(seg, j), block(seg, j), sent, mate_got.at[j], mate, rad).start()

    def finish(j):
        every = G.at[pl.ds(0, X), 0:3, pl.ds(0, bounds[j + 1] - bounds[j])]
        remote(every, every, sent, mate_got.at[j], mate, rad).wait_recv()

        for t in range(bounds[j], bounds[j + 1]):
            step(t)

    for k in range(1, X):
        seg = source(k, c)
        copy = remote(G.at[seg, 3], G.at[seg, 3], sent, dens_got.at[k - 1], mate, rad)
        copy.wait_recv()
        remote(G.at[seg, 3], G.at[seg, 3], sent, dens_mate, mate, rad).start()
    take(1)
    take(0)
    dens = G.at[pl.ds(0, X), 3]
    remote(dens, dens, sent, dens_mate, mate, rad).wait_recv()
    order = [1, 0] + list(range(2, K))
    for i, j in enumerate(order):
        if i > 0 and i + 1 < K:
            take(order[i + 1])
        finish(j)

    for way in range(2):
        @pl.when(sends[way])
        def _():
            edge_copy(way).wait_send()
    remote(ZS, ZS, side_sent, side_got, mate, rad).wait_send()
    fixes = FX.at[pl.ds(0, X - 1)]
    remote(fixes, fixes, fix_sent, side_got, mate, rad).wait_send()
    every = G.at[pl.ds(0, 2 * X - 1)]
    remote(every, every, sent, side_got, mate, rad).wait_send()


def shards(fields, shifts, courant):
    n, rn = lax.axis_size("az"), lax.axis_size("rad")
    F, T, R, L = fields.shape
    X = n // 2
    bounds = sorted({T * b // BOUNDS[-1] for b in BOUNDS})
    K, fill = len(bounds) - 1, bounds[1]
    packs, fixes = -(-3 * T // L), -(-6 * fill // L)
    tile = R * L
    held = (n + 2) * F * T * tile + 3 * fill * tile + 2 * 3 * T * L + (4 * packs + n * fixes) * tile + 9 * T * tile
    grant = 4 * held + (2 << 20)
    dma = pltpu.SemaphoreType.DMA
    vmem = pl.BlockSpec(memory_space=pltpu.VMEM)
    return pl.pallas_call(
        functools.partial(kernel, n, rn, bounds),
        out_shape=jax.ShapeDtypeStruct(fields.shape, jnp.float32),
        in_specs=[pl.BlockSpec(memory_space=pltpu.HBM)] * 3,
        out_specs=vmem,
        scratch_shapes=[
            pltpu.VMEM((3, T, R, L), jnp.float32),
            pltpu.VMEM((3, fill, R, L), jnp.float32),
            pltpu.VMEM((n, F, T, R, L), jnp.float32),
            pltpu.VMEM((2, 3, T, L), jnp.float32),
            pltpu.VMEM((2, packs, R, L), jnp.float32),
            pltpu.VMEM((2, packs, R, L), jnp.float32),
            pltpu.VMEM((n, fixes, R, L), jnp.float32),
            pltpu.VMEM((T, 4, R, L), jnp.int32),
            pltpu.VMEM((T, 4, R, L), jnp.int32),
            pltpu.VMEM((T, R, L), jnp.float32),
            pltpu.VMEM((R, T), jnp.int32),
            pltpu.VMEM((R, T), jnp.float32),
            dma((2,)), dma((2,)),
            dma(()), dma((2,)), dma((2,)), dma(()), dma(()), dma(()), dma((X - 1,)),
            dma((X - 1,)), dma(()), dma((K, X - 1)), dma((K,)),
        ],
        compiler_params=pltpu.CompilerParams(collective_id=0, has_side_effects=True, vmem_limit_bytes=grant),
    )(*(pltpu.with_memory_space_constraint(v, pltpu.HBM) for v in (fields, shifts.T, courant.T)))


def solution(mesh):
    return jax.shard_map(
        shards,
        mesh=mesh,
        in_specs=(P(None, None, "rad", "az"), P(None, "rad"), P(None, "rad")),
        out_specs=P(None, None, "rad", "az"),
        check_vma=False,
    )
```

```python
import functools
import math

import jax
import jax.numpy as jnp
from jax import lax
from jax.experimental import pallas as pl
from jax.experimental.pallas import tpu as pltpu
from jax.sharding import PartitionSpec as P

inner_radius = 0.4
adiabatic = 1.4
MESH = pl.DeviceIdType.MESH
OFFSETS = (-2, -1, 0, 1)
BOUNDS = (0, 8, 14, 16)


def remote(src, dst, send, recv, az, rad):
    return pltpu.make_async_remote_copy(
        src_ref=src,
        dst_ref=dst,
        send_sem=send,
        recv_sem=recv,
        device_id={"az": az, "rad": rad},
        device_id_type=MESH,
    )


def minmod(a, b):
    return jnp.maximum(jnp.minimum(a, b), 0.0) + jnp.minimum(jnp.maximum(a, b), 0.0)


def kernel(n, rn, bounds, fields, shifts_in, courant_in, out, raw, early, G, H, ZS, ZR, FX, SEG, LANE, CA, shifts, courant,
           local_sem, small_sem, sent, aux_sent, halo_got, fix_got, dens_got, got, mate_got):
    F, T, R, L = fields.shape
    X = n // 2
    K = len(bounds) - 1
    fill = bounds[1]
    az = lax.axis_index("az")
    rad = lax.axis_index("rad")
    x, c = az // 2, az % 2
    mate = x * 2 + (1 - c)
    before, after = lax.rem(az + n - 1, n), lax.rem(az + 1, n)

    def tiles(m):
        for a in range(1, n + 1):
            for b in range(1, F + 1):
                if m % (a * b) == 0 and m // (a * b) <= T:
                    return G.at[pl.ds(0, a), pl.ds(0, b), pl.ds(0, m // (a * b))]
        raise ValueError(m)

    def column(k, core=None):
        return lax.rem(x + k, X) * 2 + (c if core is None else core)

    def source(k, core):
        return lax.rem(x + X - k, X) * 2 + core

    has_low, has_high = rad > 0, rad < rn - 1
    sends = (has_high, has_low)
    receives = (has_low, has_high)
    toward = (rad + 1, rad - 1)

    barrier = pltpu.get_barrier_semaphore()

    def greet(a, r):
        pl.semaphore_signal(barrier, inc=1, device_id={"az": a, "rad": r}, device_id_type=MESH)

    greet(mate, rad)
    for k in range(1, X):
        greet(column(k), rad)
        greet(column(k, 1 - c), rad)
    for way in range(2):
        @pl.when(sends[way])
        def _():
            greet(az, toward[way])

    small = (
        pltpu.make_async_copy(shifts_in, shifts, small_sem.at[0]),
        pltpu.make_async_copy(courant_in, courant, small_sem.at[1]),
    )
    local = (
        pltpu.make_async_copy(fields.at[0:3], raw, local_sem),
        pltpu.make_async_copy(fields.at[3], G.at[az, 3], local_sem),
    )
    for copy in small + local:
        copy.start()

    phi_count, rad_count = n * L, rn * R
    phi_step = 2.0 * math.pi / phi_count
    rad_step = 1.0 / rad_count
    spacing = min(rad_step, inner_radius * phi_step)
    dt = 0.2 * spacing
    viscosity = 0.05 * spacing * spacing / dt
    row = lax.broadcasted_iota(jnp.int32, (R, L), 0)
    lane = lax.broadcasted_iota(jnp.int32, (R, L), 1)
    radius = inner_radius + ((rad * R + row).astype(jnp.float32) + 0.5) * (1.0 / rad_count)
    width = radius * phi_step
    inv_r = 1.0 / radius
    inv_w = 1.0 / width
    spread_az = (dt * viscosity) * inv_w * inv_w
    spread_rad = dt * viscosity / (rad_step * rad_step)
    press_rad = dt * (adiabatic - 1.0) * 0.5 / rad_step
    press_az = (dt * (adiabatic - 1.0) * 0.5) * inv_w
    turn = dt * inv_r
    pull = dt * inv_r * inv_r
    heat = dt * (adiabatic - 1.0)
    heat_rad = heat * 0.5 / rad_step
    heat_az = (heat * 0.5) * inv_w
    heat_r = heat * inv_r
    bits = L.bit_length() - 1
    first_lane, last_lane = lane == 0, lane == L - 1
    first_row, last_row = row == 0, row == R - 1

    def turned(value, amount):
        return pltpu.roll(value, amount % L, 1) if amount % L else value

    for copy in small:
        copy.wait()
    for t in range(T):
        moves = jnp.broadcast_to(shifts[:, t : t + 1], (R, L))
        cour = jnp.broadcast_to(courant[:, t : t + 1], (R, L))
        CA[t] = jnp.abs(cour)
        sign = jnp.where(cour >= 0.0, 1, -1)
        for o, offset in enumerate(OFFSETS):
            s = moves - sign * offset
            s = jnp.where(s < 0, s + phi_count, s)
            s = jnp.where(s >= phi_count, s - phi_count, s)
            q = s >> bits
            rest = s & (L - 1)
            seg = az - q - jnp.where(lane + rest >= L, 1, 0)
            SEG[t, o] = jnp.where(seg < 0, seg + n, seg)
            LANE[t, o] = (lane - rest) & (L - 1)

    pltpu.make_async_copy(fields, G.at[0], local_sem).wait()

    for side in range(2):
        for p in range(ZS.shape[1]):
            packed = jnp.zeros((R, L), jnp.float32)
            for i in range(p * L, min(3 * T, (p + 1) * L)):
                packed = jnp.where(lane == i - p * L, turned(raw[i // T, i % T], i - p * L + side), packed)
            ZS[side, p] = packed

    for way in range(2):
        @pl.when(jnp.logical_not(receives[way]))
        def _():
            H[way] = raw[:, :, (R - 1) * way, :]

    def stencil(t, dst, inner):
        vr, vp, en, den = raw[0, t], raw[1, t], raw[2, t], G[az, 3, t]

        def around(f, q):
            i = f * T + t
            left, right = turned(q, 1), turned(q, L - 1)
            low, high = pltpu.roll(q, 1, 0), pltpu.roll(q, R - 1, 0)
            if not inner:
                left = jnp.where(first_lane, turned(ZR[0, i // L], -i), left)
                right = jnp.where(last_lane, turned(ZR[1, i // L], L - 1 - i), right)
                low = jnp.where(first_row, H[0, f, pl.ds(t, 1), :], low)
                high = jnp.where(last_row, H[1, f, pl.ds(t, 1), :], high)
            return left, right, low, high

        vl, vh, vd, vu = around(0, vr)
        pl_, ph, pd, pu = around(1, vp)
        el, eh, ed, eu = around(2, en)
        inv_den = 1.0 / den
        dst[0, t] = vr + (
            spread_az * (vh + vl - 2.0 * vr)
            + spread_rad * (vu + vd - 2.0 * vr)
            + (vp * vp * turn - pull)
            - press_rad * (eu - ed) * inv_den
        )
        dst[1, t] = vp + (
            spread_az * (ph + pl_ - 2.0 * vp)
            + spread_rad * (pu + pd - 2.0 * vp)
            - vr * vp * turn
            - press_az * (eh - el) * inv_den
        )
        dst[2, t] = en - en * (heat_rad * (vu - vd) + heat_az * (ph - pl_) + heat_r * vr)

    neighbours = has_low.astype(jnp.int32) + has_high.astype(jnp.int32)
    pl.semaphore_wait(barrier, 2 * X - 1 + neighbours)

    def side_copy(side):
        return remote(ZS.at[side], ZR.at[1 - side], aux_sent, halo_got, after if side else before, rad)

    def edge_copy(way):
        return remote(raw.at[:, :, (R - 1) * (1 - way), :], H.at[way], aux_sent, halo_got, az, toward[way])

    def block(seg, j):
        return G.at[seg, 0:3, pl.ds(bounds[j], bounds[j + 1] - bounds[j])]

    for side in range(2):
        side_copy(side).start()
    for way in range(2):
        @pl.when(sends[way])
        def _():
            edge_copy(way).start()
    for k in range(1, X):
        remote(G.at[az, 3], G.at[az, 3], sent, dens_got.at[k - 1], column(k), rad).start()
    for t in range(fill):
        stencil(t, early, True)

    for k in range(1, X):
        inside = pl.ds(1, R - 2)
        remote(early.at[:, :, inside], G.at[az, 0:3, pl.ds(0, fill), inside], sent, got.at[0, k - 1], column(k), rad).start()
    for count in range(3):
        @pl.when(neighbours == count)
        def _():
            came = tiles(2 * ZR.shape[1] + count * 3 * T // R)
            remote(came, came, aux_sent, halo_got, mate, rad).wait_recv()

    for j in range(K):
        for t in range(bounds[j], bounds[j + 1]):
            stencil(t, G.at[az], False)
        if j == 0:
            for p in range(FX.shape[1]):
                packed = jnp.zeros((R, L), jnp.float32)
                for i in range(p * L, min(6 * fill, (p + 1) * L)):
                    f, t, side = i // (2 * fill), i // 2 % fill, i % 2
                    packed = jnp.where(lane == i - p * L, turned(G[az, f, t], i - p * L + side), packed)
                FX[az, p] = packed
            for k in range(1, X):
                for r in (0, R - 1):
                    line = G.at[az, 0:3, pl.ds(0, fill), r]
                    remote(line, line, sent, got.at[0, k - 1], column(k), rad).start()
                remote(FX.at[az], FX.at[az], aux_sent, fix_got.at[k - 1], column(k), rad).start()
        else:
            for k in range(1, X):
                remote(block(az, j), block(az, j), sent, got.at[j, k - 1], column(k), rad).start()
                if j == K - 1:
                    remote(block(az, j), block(az, j), sent, mate_got.at[j], column(k, 1 - c), rad).start()
    remote(G.at[az, 3], G.at[az, 3], sent, mate_got.at[0], mate, rad).start()
    for j in range(K):
        remote(block(az, j), block(az, j), sent, mate_got.at[j], mate, rad).start()

    def step(t):
        amount = CA[t]
        half = 0.5 * (1.0 - amount)
        taken = [[] for _ in range(4)]
        moved = [[G[s, f, t] for f in range(4)] for s in range(n)]
        for o in range(len(OFFSETS)):
            seg, at = SEG[t, o], LANE[t, o]
            chosen = [seg == s for s in range(n - 1)]
            for f in range(4):
                value = moved[n - 1][f]
                for s in range(n - 1):
                    value = jnp.where(chosen[s], moved[s][f], value)
                taken[f].append(jnp.take_along_axis(value, at, axis=1, mode="promise_in_bounds"))
        for f in range(4):
            q0, q1, q2, q3 = taken[f]
            d0, d1, d2 = q1 - q0, q2 - q1, q3 - q2
            enters = q1 + half * minmod(d0, d1)
            leaves = q2 + half * minmod(d1, d2)
            out[f, t] = q2 - amount * (leaves - enters)

    def take(j):
        for k in range(1, X):
            seg = source(k, c)
            copy = remote(block(seg, j), block(seg, j), sent, got.at[j, k - 1], mate, rad)
            copy.wait_recv()
            if j == 0:
                remote(FX.at[seg], FX.at[seg], aux_sent, fix_got.at[k - 1], mate, rad).wait_recv()
                for i in range(3 * fill):
                    f, t = i // fill, i % fill
                    p, at = 2 * i // L, 2 * i % L
                    value = jnp.where(first_lane, turned(FX[seg, p], -at), G[seg, f, t])
                    G[seg, f, t] = jnp.where(last_lane, turned(FX[seg, p], L - 2 - at), value)
            if j < K - 1:
                remote(block(seg, j), block(seg, j), sent, mate_got.at[j], mate, rad).start()

    def finish(j):
        came = tiles(X * (3 * (bounds[j + 1] - bounds[j]) + (0 if j else T)))
        remote(came, came, sent, mate_got.at[j], mate, rad).wait_recv()

        for t in range(bounds[j], bounds[j + 1]):
            step(t)

    for k in range(1, X):
        seg = source(k, c)
        copy = remote(G.at[seg, 3], G.at[seg, 3], sent, dens_got.at[k - 1], mate, rad)
        copy.wait_recv()
        remote(G.at[seg, 3], G.at[seg, 3], sent, mate_got.at[0], mate, rad).start()
    take(0)
    take(1)
    for j in range(K - 2):
        if j > 0:
            take(j + 1)
        finish(j)
    take(K - 1)
    finish(K - 1)
    finish(K - 2)

    for count in range(3):
        @pl.when(neighbours == count)
        def _():
            gone = tiles(2 * ZR.shape[1] + (X - 1) * FX.shape[1] + count * 3 * T // R)
            remote(gone, gone, aux_sent, halo_got, mate, rad).wait_send()
    every = G.at[pl.ds(0, 2 * X - 1)]
    remote(every, every, sent, halo_got, mate, rad).wait_send()


def shards(fields, shifts, courant):
    n, rn = lax.axis_size("az"), lax.axis_size("rad")
    F, T, R, L = fields.shape
    X = n // 2
    bounds = sorted({T * b // BOUNDS[-1] for b in BOUNDS})
    K, fill = len(bounds) - 1, bounds[1]
    packs, fixes = -(-3 * T // L), -(-6 * fill // L)
    tile = R * L
    held = (n + 2) * F * T * tile + 3 * fill * tile + 2 * 3 * T * L + (4 * packs + n * fixes) * tile + 9 * T * tile
    grant = 4 * held + (2 << 20)
    dma = pltpu.SemaphoreType.DMA
    vmem = pl.BlockSpec(memory_space=pltpu.VMEM)
    return pl.pallas_call(
        functools.partial(kernel, n, rn, bounds),
        out_shape=jax.ShapeDtypeStruct(fields.shape, jnp.float32),
        in_specs=[pl.BlockSpec(memory_space=pltpu.HBM)] * 3,
        out_specs=vmem,
        scratch_shapes=[
            pltpu.VMEM((3, T, R, L), jnp.float32),
            pltpu.VMEM((3, fill, R, L), jnp.float32),
            pltpu.VMEM((n, F, T, R, L), jnp.float32),
            pltpu.VMEM((2, 3, T, L), jnp.float32),
            pltpu.VMEM((2, packs, R, L), jnp.float32),
            pltpu.VMEM((2, packs, R, L), jnp.float32),
            pltpu.VMEM((n, fixes, R, L), jnp.float32),
            pltpu.VMEM((T, 4, R, L), jnp.int32),
            pltpu.VMEM((T, 4, R, L), jnp.int32),
            pltpu.VMEM((T, R, L), jnp.float32),
            pltpu.VMEM((R, T), jnp.int32),
            pltpu.VMEM((R, T), jnp.float32),
            dma(()), dma((2,)), dma(()), dma(()), dma(()),
            dma((X - 1,)), dma((X - 1,)), dma((K, X - 1)), dma((K,)),
        ],
        compiler_params=pltpu.CompilerParams(collective_id=0, has_side_effects=True, vmem_limit_bytes=grant),
    )(*(pltpu.with_memory_space_constraint(v, pltpu.HBM) for v in (fields, shifts.T, courant.T)))


def solution(mesh):
    return jax.shard_map(
        shards,
        mesh=mesh,
        in_specs=(P(None, None, "rad", "az"), P(None, "rad"), P(None, "rad")),
        out_specs=P(None, None, "rad", "az"),
        check_vma=False,
    )
```

```python
import functools
import math

import jax
import jax.numpy as jnp
from jax import lax
from jax.experimental import pallas as pl
from jax.experimental.pallas import tpu as pltpu
from jax.sharding import PartitionSpec as P

inner_radius = 0.4
adiabatic = 1.4
MESH = pl.DeviceIdType.MESH
OFFSETS = (-2, -1, 0, 1)
BOUNDS = (0, 8, 12, 16)


def remote(src, dst, send, recv, az, rad):
    return pltpu.make_async_remote_copy(
        src_ref=src,
        dst_ref=dst,
        send_sem=send,
        recv_sem=recv,
        device_id={"az": az, "rad": rad},
        device_id_type=MESH,
    )


def minmod(a, b):
    return jnp.maximum(jnp.minimum(a, b), 0.0) + jnp.minimum(jnp.maximum(a, b), 0.0)


def kernel(n, rn, bounds, fields, shifts_in, courant_in, out, raw, early, D, G, H, ZS, ZR, FX, SEG, LANE, CA, shifts, courant,
           local_sem, small_sem, sent, aux_sent, halo_got, got, mate_got):
    _, T, R, L = fields.shape
    X = n // 2
    K = len(bounds) - 1
    fill = bounds[1]
    az = lax.axis_index("az")
    rad = lax.axis_index("rad")
    x, c = az // 2, az % 2
    mate = x * 2 + (1 - c)
    before, after = lax.rem(az + n - 1, n), lax.rem(az + 1, n)

    def column(k, core=None):
        return lax.rem(x + k, X) * 2 + (c if core is None else core)

    def source(k, core):
        return lax.rem(x + X - k, X) * 2 + core

    def tiles(m):
        return G.at[pl.ds(0, m)]

    def dens(seg):
        return D.at[pl.ds(seg * T, T)]

    has_low, has_high = rad > 0, rad < rn - 1
    sends = (has_high, has_low)
    receives = (has_low, has_high)
    toward = (rad + 1, rad - 1)
    neighbours = has_low.astype(jnp.int32) + has_high.astype(jnp.int32)

    barrier = pltpu.get_barrier_semaphore()

    def greet(sem, a, r):
        pl.semaphore_signal(sem, inc=1, device_id={"az": a, "rad": r}, device_id_type=MESH)

    greet(barrier, mate, rad)
    for k in range(1, X):
        greet(barrier, column(k), rad)
        greet(barrier, column(k, 1 - c), rad)
    for way in range(2):
        @pl.when(sends[way])
        def _():
            greet(barrier, az, toward[way])

    small = (
        pltpu.make_async_copy(shifts_in, shifts, small_sem),
        pltpu.make_async_copy(courant_in, courant.at[0], small_sem),
    )
    local = (
        pltpu.make_async_copy(fields.at[0:3], raw, local_sem),
        pltpu.make_async_copy(fields.at[3], dens(az), local_sem),
    )
    for copy in small + local:
        copy.start()

    def density_out(from_ref):
        for k in range(1, X):
            remote(from_ref, dens(az), aux_sent, got.at[0, k - 1], column(k), rad).start()

    def edge_copy(way, from_ref):
        return remote(from_ref.at[:, :, (R - 1) * (1 - way), :], H.at[way], aux_sent, halo_got, az, toward[way])

    def edges_out(rows):
        for way in range(2):
            pl.when(sends[way])(edge_copy(way, rows).start)

    phi_count, rad_count = n * L, rn * R
    phi_step = 2.0 * math.pi / phi_count
    rad_step = 1.0 / rad_count
    spacing = min(rad_step, inner_radius * phi_step)
    dt = 0.2 * spacing
    viscosity = 0.05 * spacing * spacing / dt
    row = lax.broadcasted_iota(jnp.int32, (R, L), 0)
    lane = lax.broadcasted_iota(jnp.int32, (R, L), 1)
    radius = inner_radius + ((rad * R + row).astype(jnp.float32) + 0.5) * (1.0 / rad_count)
    width = radius * phi_step
    inv_r = 1.0 / radius
    inv_w = 1.0 / width
    spread_az = (dt * viscosity) * inv_w * inv_w
    spread_rad = dt * viscosity / (rad_step * rad_step)
    press_rad = dt * (adiabatic - 1.0) * 0.5 / rad_step
    press_az = (dt * (adiabatic - 1.0) * 0.5) * inv_w
    turn = dt * inv_r
    pull = dt * inv_r * inv_r
    heat = dt * (adiabatic - 1.0)
    heat_rad = heat * 0.5 / rad_step
    heat_az = (heat * 0.5) * inv_w
    heat_r = heat * inv_r
    bits = L.bit_length() - 1
    first_lane, last_lane = lane == 0, lane == L - 1
    first_row, last_row = row == 0, row == R - 1

    def turned(value, amount):
        return pltpu.roll(value, amount % L, 1) if amount % L else value

    pltpu.make_async_copy(tiles(4 * T), tiles(4 * T), local_sem).wait()

    for side in range(2):
        for p in range(ZS.shape[1]):
            packed = jnp.zeros((R, L), jnp.float32)
            for i in range(p * L, min(3 * T, (p + 1) * L)):
                packed = jnp.where(lane == i - p * L, turned(raw[i // T, i % T], i - p * L + side), packed)
            ZS[side, p] = packed

    for way in range(2):
        @pl.when(jnp.logical_not(receives[way]))
        def _():
            H[way] = raw[:, :, (R - 1) * way, :]

    def stencil(t, inner):
        vr, vp, en, den = raw[0, t], raw[1, t], raw[2, t], D[az * T + t]

        def around(f, q):
            i = f * T + t
            left, right = turned(q, 1), turned(q, L - 1)
            low, high = pltpu.roll(q, 1, 0), pltpu.roll(q, R - 1, 0)
            if not inner:
                left = jnp.where(first_lane, turned(ZR[0, i // L], -i), left)
                right = jnp.where(last_lane, turned(ZR[1, i // L], L - 1 - i), right)
                low = jnp.where(first_row, H[0, f, pl.ds(t, 1), :], low)
                high = jnp.where(last_row, H[1, f, pl.ds(t, 1), :], high)
            return left, right, low, high

        vl, vh, vd, vu = around(0, vr)
        pl_, ph, pd, pu = around(1, vp)
        el, eh, ed, eu = around(2, en)
        inv_den = 1.0 / den
        new_r = vr + (
            spread_az * (vh + vl - 2.0 * vr)
            + spread_rad * (vu + vd - 2.0 * vr)
            + (vp * vp * turn - pull)
            - press_rad * (eu - ed) * inv_den
        )
        new_p = vp + (
            spread_az * (ph + pl_ - 2.0 * vp)
            + spread_rad * (pu + pd - 2.0 * vp)
            - vr * vp * turn
            - press_az * (eh - el) * inv_den
        )
        new_e = en - en * (heat_rad * (vu - vd) + heat_az * (ph - pl_) + heat_r * vr)
        return new_r, new_p, new_e

    def place(seg, t):
        return (seg * T + t) * 3

    def block(seg, j):
        return G.at[pl.ds(place(seg, bounds[j]), 3 * (bounds[j + 1] - bounds[j]))]

    def side_copy(side):
        return remote(ZS.at[side], ZR.at[1 - side], aux_sent, halo_got, after if side else before, rad)

    pl.semaphore_wait(barrier, 2 * X - 1 + neighbours)

    for side in range(2):
        side_copy(side).start()

    edges_out(raw)

    density_out(dens(az))

    for t in range(fill):
        for f, value in enumerate(stencil(t, True)):
            early[3 * t + f] = value
    for k in range(1, X):
        inside = pl.ds(1, R - 2)
        remote(early.at[:, inside], G.at[pl.ds(place(az, 0), 3 * fill), inside], sent, got.at[0, k - 1], column(k), rad).start()

    pltpu.make_async_copy(courant, courant, small_sem).wait()
    for t in range(T):
        moves = jnp.broadcast_to(shifts[:, t : t + 1], (R, L))
        cour = jnp.broadcast_to(courant[0, :, t : t + 1], (R, L))
        CA[t] = jnp.abs(cour)
        sign = jnp.where(cour >= 0.0, 1, -1)
        for o, offset in enumerate(OFFSETS):
            s = moves - sign * offset
            s = jnp.where(s < 0, s + phi_count, s)
            s = jnp.where(s >= phi_count, s - phi_count, s)
            q = s >> bits
            rest = s & (L - 1)
            seg = az - q - jnp.where(lane + rest >= L, 1, 0)
            SEG[t, o] = jnp.where(seg < 0, seg + n, seg)
            LANE[t, o] = (lane - rest) & (L - 1)

    for count in range(3):
        @pl.when(neighbours == count)
        def _():
            came = tiles(2 * ZR.shape[1] + count * 3 * T // R)
            remote(came, came, aux_sent, halo_got, mate, rad).wait_recv()

    for j in range(K):
        for t in range(bounds[j], bounds[j + 1]):
            for f, value in enumerate(stencil(t, False)):
                G[place(az, t) + f] = value
        if j == 0:
            for p in range(FX.shape[1]):
                packed = jnp.zeros((R, L), jnp.float32)
                for i in range(p * L, min(6 * fill, (p + 1) * L)):
                    packed = jnp.where(lane == i - p * L, turned(G[place(az, 0) + i // 2], i - p * L + i % 2), packed)
                FX[az, p] = packed
            for k in range(1, X):
                for r in (0, R - 1):
                    line = G.at[pl.ds(place(az, 0), 3 * fill), r]
                    remote(line, line, sent, got.at[0, k - 1], column(k), rad).start()
                remote(FX.at[az], FX.at[az], aux_sent, got.at[0, k - 1], column(k), rad).start()
        else:
            for k in range(1, X):
                remote(block(az, j), block(az, j), sent, got.at[j, k - 1], column(k), rad).start()
                if j == K - 1:
                    direct = remote(block(az, j), block(az, j), sent, mate_got.at[j], column(k, 1), rad)
                    pl.when(c == 0)(direct.start)
    remote(dens(az), dens(az), aux_sent, mate_got.at[0], mate, rad).start()
    for j in range(K):
        remote(block(az, j), block(az, j), sent, mate_got.at[j], mate, rad).start()

    def step(t):
        amount = CA[t]
        half = 0.5 * (1.0 - amount)
        taken = [[] for _ in range(4)]
        moved = [[G[place(s, t) + f] for f in range(3)] + [D[s * T + t]] for s in range(n)]
        for o in range(len(OFFSETS)):
            seg, at = SEG[t, o], LANE[t, o]
            chosen = [seg == s for s in range(n - 1)]
            for f in range(4):
                value = moved[n - 1][f]
                for s in range(n - 1):
                    value = jnp.where(chosen[s], moved[s][f], value)
                taken[f].append(jnp.take_along_axis(value, at, axis=1, mode="promise_in_bounds"))
        for f in range(4):
            q0, q1, q2, q3 = taken[f]
            d0, d1, d2 = q1 - q0, q2 - q1, q3 - q2
            enters = q1 + half * minmod(d0, d1)
            leaves = q2 + half * minmod(d1, d2)
            out[f, t] = q2 - amount * (leaves - enters)

    def take(j, forward=True):
        for k in range(1, X):
            seg = source(k, c)
            came = tiles(3 * (bounds[j + 1] - bounds[j]) + (0 if j else T + FX.shape[1]))
            remote(came, came, sent, got.at[j, k - 1], mate, rad).wait_recv()
            if j == 0:
                for i in range(3 * fill):
                    p, at = 2 * i // L, 2 * i % L
                    value = jnp.where(first_lane, turned(FX[seg, p], -at), G[place(seg, 0) + i])
                    G[place(seg, 0) + i] = jnp.where(last_lane, turned(FX[seg, p], L - 2 - at), value)
                remote(dens(seg), dens(seg), aux_sent, mate_got.at[0], mate, rad).start()
            if forward:
                remote(block(seg, j), block(seg, j), sent, mate_got.at[j], mate, rad).start()

    def finish(j):
        came = tiles(X * (3 * (bounds[j + 1] - bounds[j]) + (0 if j else T)))
        remote(came, came, sent, mate_got.at[j], mate, rad).wait_recv()
        for t in range(bounds[j], bounds[j + 1]):
            step(t)

    @pl.when(c == 1)
    def _():
        for j in range(K):
            take(j)

    for j in range(K):
        @pl.when(c == 0)
        def _():
            take(j, j < K - 1)

        finish(j)

    for count in range(3):
        @pl.when(neighbours == count)
        def _():
            gone = tiles(2 * ZR.shape[1] + (2 * X - 1) * T + (X - 1) * FX.shape[1] + count * 3 * T // R)
            remote(gone, gone, aux_sent, halo_got, mate, rad).wait_send()
    gone = tiles((2 * X - 1) * 3 * T)
    remote(gone, gone, sent, halo_got, mate, rad).wait_send()


def shards(fields, shifts, courant):
    n, rn = lax.axis_size("az"), lax.axis_size("rad")
    F, T, R, L = fields.shape
    X = n // 2
    bounds = sorted({T * b // BOUNDS[-1] for b in BOUNDS})
    K, fill = len(bounds) - 1, bounds[1]
    packs, fixes = -(-3 * T // L), -(-6 * fill // L)
    tile = R * L
    held = (n + 2) * F * T * tile + 3 * fill * tile + 2 * 3 * T * L + (4 * packs + n * fixes) * tile + 9 * T * tile
    grant = 4 * held + (2 << 20)
    dma = pltpu.SemaphoreType.DMA
    vmem = pl.BlockSpec(memory_space=pltpu.VMEM)
    return pl.pallas_call(
        functools.partial(kernel, n, rn, bounds),
        out_shape=jax.ShapeDtypeStruct(fields.shape, jnp.float32),
        in_specs=[pl.BlockSpec(memory_space=pltpu.HBM)] * 3,
        out_specs=vmem,
        scratch_shapes=[
            pltpu.VMEM((3, T, R, L), jnp.float32),
            pltpu.VMEM((3 * fill, R, L), jnp.float32),
            pltpu.VMEM((n * T, R, L), jnp.float32),
            pltpu.VMEM((n * T * 3, R, L), jnp.float32),
            pltpu.VMEM((2, 3, T, L), jnp.float32),
            pltpu.VMEM((2, packs, R, L), jnp.float32),
            pltpu.VMEM((2, packs, R, L), jnp.float32),
            pltpu.VMEM((n, fixes, R, L), jnp.float32),
            pltpu.VMEM((T, 4, R, L), jnp.int32),
            pltpu.VMEM((T, 4, R, L), jnp.int32),
            pltpu.VMEM((T, R, L), jnp.float32),
            pltpu.VMEM((R, T), jnp.int32),
            pltpu.VMEM((2, R, T), jnp.float32),
            dma(()), dma(()), dma(()), dma(()), dma(()),
            dma((K, X - 1)), dma((K,)),
        ],
        compiler_params=pltpu.CompilerParams(collective_id=0, has_side_effects=True, vmem_limit_bytes=grant),
    )(*(pltpu.with_memory_space_constraint(v, pltpu.HBM) for v in (fields, shifts.T, courant.T)))


def solution(mesh):
    return jax.shard_map(
        shards,
        mesh=mesh,
        in_specs=(P(None, None, "rad", "az"), P(None, "rad"), P(None, "rad")),
        out_specs=P(None, None, "rad", "az"),
        check_vma=False,
    )
```

```python
import functools
import math

import jax
import jax.numpy as jnp
from jax import lax
from jax.experimental import pallas as pl
from jax.experimental.pallas import tpu as pltpu
from jax.sharding import PartitionSpec as P

inner_radius = 0.4
adiabatic = 1.4
MESH = pl.DeviceIdType.MESH
OFFSETS = (-2, -1, 0, 1)
BOUNDS = (0, 8, 11, 16)


def remote(src, dst, send, recv, az, rad):
    return pltpu.make_async_remote_copy(
        src_ref=src,
        dst_ref=dst,
        send_sem=send,
        recv_sem=recv,
        device_id={"az": az, "rad": rad},
        device_id_type=MESH,
    )


def minmod(a, b):
    return jnp.maximum(jnp.minimum(a, b), jnp.minimum(jnp.maximum(a, b), 0.0))


def kernel(n, rn, bounds, fields, shifts_in, courant_in, out, raw, early, D, G, H, ZS, ZR, FX, SEG, LANE, CA, shifts, courant,
           local_sem, small_sem, sent, aux_sent, halo_got, late_got, dens_got, got, mate_got):
    _, T, R, L = fields.shape
    X = n // 2
    K = len(bounds) - 1
    fill = bounds[1]
    az = lax.axis_index("az")
    rad = lax.axis_index("rad")
    x, c = az // 2, az % 2
    mate = x * 2 + (1 - c)
    before, after = lax.rem(az + n - 1, n), lax.rem(az + 1, n)

    def column(k, core=None):
        return lax.rem(x + k, X) * 2 + (c if core is None else core)

    def source(k, core):
        return lax.rem(x + X - k, X) * 2 + core

    def tiles(m):
        return G.at[pl.ds(0, m)]

    def dens(seg):
        return D.at[pl.ds(seg * T, T)]

    has_low, has_high = rad > 0, rad < rn - 1
    sends = (has_high, has_low)
    receives = (has_low, has_high)
    toward = (rad + 1, rad - 1)
    neighbours = has_low.astype(jnp.int32) + has_high.astype(jnp.int32)

    barrier = pltpu.get_barrier_semaphore()

    def greet(sem, a, r):
        pl.semaphore_signal(sem, inc=1, device_id={"az": a, "rad": r}, device_id_type=MESH)

    greet(barrier, mate, rad)
    for k in range(1, X):
        greet(barrier, column(k), rad)
        greet(barrier, column(k, 1 - c), rad)
    for way in range(2):
        @pl.when(sends[way])
        def _():
            greet(barrier, az, toward[way])

    small = (
        pltpu.make_async_copy(shifts_in, shifts, small_sem),
        pltpu.make_async_copy(courant_in, courant.at[0], small_sem),
    )
    local = (
        pltpu.make_async_copy(fields.at[0:3], raw, local_sem),
        pltpu.make_async_copy(fields.at[3], dens(az), local_sem),
    )
    for copy in small + local:
        copy.start()

    def density_out(from_ref):
        for k in range(1, X):
            remote(from_ref, dens(az), aux_sent, dens_got.at[k - 1], column(k), rad).start()

    parts = ((0, fill, halo_got), (fill, T - fill, late_got))

    def edge_copy(way, first, count, got_sem):
        some = pl.ds(first, count)
        return remote(raw.at[:, some, (R - 1) * (1 - way), :], H.at[way, :, some], aux_sent, got_sem, az, toward[way])

    def edges_out():
        for part in parts:
            for way in range(2):
                pl.when(sends[way])(edge_copy(way, *part).start)

    phi_count, rad_count = n * L, rn * R
    phi_step = 2.0 * math.pi / phi_count
    rad_step = 1.0 / rad_count
    spacing = min(rad_step, inner_radius * phi_step)
    dt = 0.2 * spacing
    viscosity = 0.05 * spacing * spacing / dt
    row = lax.broadcasted_iota(jnp.int32, (R, L), 0)
    lane = lax.broadcasted_iota(jnp.int32, (R, L), 1)
    radius = inner_radius + ((rad * R + row).astype(jnp.float32) + 0.5) * (1.0 / rad_count)
    width = radius * phi_step
    inv_r = 1.0 / radius
    inv_w = 1.0 / width
    spread_az = (dt * viscosity) * inv_w * inv_w
    spread_rad = dt * viscosity / (rad_step * rad_step)
    press_rad = dt * (adiabatic - 1.0) * 0.5 / rad_step
    press_az = (dt * (adiabatic - 1.0) * 0.5) * inv_w
    turn = dt * inv_r
    pull = dt * inv_r * inv_r
    heat = dt * (adiabatic - 1.0)
    heat_rad = heat * 0.5 / rad_step
    heat_az = (heat * 0.5) * inv_w
    heat_r = heat * inv_r
    bits = L.bit_length() - 1
    first_lane, last_lane = lane == 0, lane == L - 1
    first_row, last_row = row == 0, row == R - 1

    def turned(value, amount):
        return pltpu.roll(value, amount % L, 1) if amount % L else value

    pltpu.make_async_copy(tiles(4 * T), tiles(4 * T), local_sem).wait()

    for side in range(2):
        for p in range(ZS.shape[1]):
            packed = jnp.zeros((R, L), jnp.float32)
            for i in range(p * L, min(3 * T, (p + 1) * L)):
                packed = jnp.where(lane == i - p * L, turned(raw[i // T, i % T], i - p * L + side), packed)
            ZS[side, p] = packed

    for way in range(2):
        @pl.when(jnp.logical_not(receives[way]))
        def _():
            H[way] = raw[:, :, (R - 1) * way, :]

    def stencil(t, inner):
        vr, vp, en, den = raw[0, t], raw[1, t], raw[2, t], D[az * T + t]

        def around(f, q):
            i = f * T + t
            left, right = turned(q, 1), turned(q, L - 1)
            low, high = pltpu.roll(q, 1, 0), pltpu.roll(q, R - 1, 0)
            if not inner:
                left = jnp.where(first_lane, turned(ZR[0, i // L], -i), left)
                right = jnp.where(last_lane, turned(ZR[1, i // L], L - 1 - i), right)
                low = jnp.where(first_row, H[0, f, pl.ds(t, 1), :], low)
                high = jnp.where(last_row, H[1, f, pl.ds(t, 1), :], high)
            return left, right, low, high

        vl, vh, vd, vu = around(0, vr)
        pl_, ph, pd, pu = around(1, vp)
        el, eh, ed, eu = around(2, en)
        inv_den = 1.0 / den
        new_r = vr + (
            spread_az * (vh + vl - 2.0 * vr)
            + spread_rad * (vu + vd - 2.0 * vr)
            + (vp * vp * turn - pull)
            - press_rad * (eu - ed) * inv_den
        )
        new_p = vp + (
            spread_az * (ph + pl_ - 2.0 * vp)
            + spread_rad * (pu + pd - 2.0 * vp)
            - vr * vp * turn
            - press_az * (eh - el) * inv_den
        )
        new_e = en - en * (heat_rad * (vu - vd) + heat_az * (ph - pl_) + heat_r * vr)
        return new_r, new_p, new_e

    def place(seg, t):
        return (seg * T + t) * 3

    def block(seg, j):
        return G.at[pl.ds(place(seg, bounds[j]), 3 * (bounds[j + 1] - bounds[j]))]

    def side_copy(side):
        return remote(ZS.at[side], ZR.at[1 - side], aux_sent, halo_got, after if side else before, rad)

    pl.semaphore_wait(barrier, 2 * X - 1 + neighbours)

    for side in range(2):
        side_copy(side).start()

    edges_out()

    density_out(dens(az))

    for t in range(fill):
        for f, value in enumerate(stencil(t, True)):
            early[3 * t + f] = value
    for k in range(1, X):
        inside = pl.ds(1, R - 2)
        remote(early.at[:, inside], G.at[pl.ds(place(az, 0), 3 * fill), inside], sent, got.at[0, k - 1], column(k), rad).start()

    pltpu.make_async_copy(courant, courant, small_sem).wait()
    for t in range(T):
        moves = jnp.broadcast_to(shifts[:, t : t + 1], (R, L))
        cour = jnp.broadcast_to(courant[0, :, t : t + 1], (R, L))
        CA[t] = jnp.abs(cour)
        sign = jnp.where(cour >= 0.0, 1, -1)
        for o, offset in enumerate(OFFSETS):
            s = moves - sign * offset
            s = jnp.where(s < 0, s + phi_count, s)
            s = jnp.where(s >= phi_count, s - phi_count, s)
            q = s >> bits
            rest = s & (L - 1)
            seg = az - q - jnp.where(lane + rest >= L, 1, 0)
            SEG[t, o] = jnp.where(seg < 0, seg + n, seg)
            LANE[t, o] = (lane - rest) & (L - 1)

    for count in range(3):
        @pl.when(neighbours == count)
        def _():
            came = tiles(2 * ZR.shape[1] + count * 3 * fill // R)
            remote(came, came, aux_sent, halo_got, mate, rad).wait_recv()

    for j in range(K):
        if j == 1:
            for count in range(1, 3):
                @pl.when(neighbours == count)
                def _():
                    came = tiles(count * 3 * (T - fill) // R)
                    remote(came, came, aux_sent, late_got, mate, rad).wait_recv()

        for t in range(bounds[j], bounds[j + 1]):
            for f, value in enumerate(stencil(t, False)):
                G[place(az, t) + f] = value
        if j == 0:
            for p in range(FX.shape[1]):
                packed = jnp.zeros((R, L), jnp.float32)
                for i in range(p * L, min(6 * fill, (p + 1) * L)):
                    packed = jnp.where(lane == i - p * L, turned(G[place(az, 0) + i // 2], i - p * L + i % 2), packed)
                FX[az, p] = packed
            for k in range(1, X):
                for r in (0, R - 1):
                    line = G.at[pl.ds(place(az, 0), 3 * fill), r]
                    remote(line, line, sent, got.at[0, k - 1], column(k), rad).start()
                remote(FX.at[az], FX.at[az], aux_sent, got.at[0, k - 1], column(k), rad).start()
        else:
            for k in range(1, X):
                remote(block(az, j), block(az, j), sent, got.at[j, k - 1], column(k), rad).start()
                if j == K - 1:
                    direct = remote(block(az, j), block(az, j), sent, mate_got.at[j], column(k, 1), rad)
                    pl.when(c == 0)(direct.start)
    remote(dens(az), dens(az), aux_sent, mate_got.at[0], mate, rad).start()
    for j in range(K):
        remote(block(az, j), block(az, j), sent, mate_got.at[j], mate, rad).start()

    def step(t):
        amount = CA[t]
        half = 0.5 * (1.0 - amount)
        taken = [[] for _ in range(4)]
        moved = [[G[place(s, t) + f] for f in range(3)] + [D[s * T + t]] for s in range(n)]
        for o in range(len(OFFSETS)):
            seg, at = SEG[t, o], LANE[t, o]
            chosen = [seg == s for s in range(n - 1)]
            for f in range(4):
                value = moved[n - 1][f]
                for s in range(n - 1):
                    value = jnp.where(chosen[s], moved[s][f], value)
                taken[f].append(jnp.take_along_axis(value, at, axis=1, mode="promise_in_bounds"))
        for f in range(4):
            q0, q1, q2, q3 = taken[f]
            d0, d1, d2 = q1 - q0, q2 - q1, q3 - q2
            enters = q1 + half * minmod(d0, d1)
            leaves = q2 + half * minmod(d1, d2)
            out[f, t] = q2 - amount * (leaves - enters)

    def take(j, forward=True):
        for k in range(1, X):
            seg = source(k, c)
            came = tiles(3 * (bounds[j + 1] - bounds[j]) + (0 if j else FX.shape[1]))
            remote(came, came, sent, got.at[j, k - 1], mate, rad).wait_recv()
            if j == 0:
                for i in range(3 * fill):
                    p, at = 2 * i // L, 2 * i % L
                    value = jnp.where(first_lane, turned(FX[seg, p], -at), G[place(seg, 0) + i])
                    G[place(seg, 0) + i] = jnp.where(last_lane, turned(FX[seg, p], L - 2 - at), value)
            if forward:
                remote(block(seg, j), block(seg, j), sent, mate_got.at[j], mate, rad).start()

    def finish(j):
        came = tiles(X * (3 * (bounds[j + 1] - bounds[j]) + (0 if j else T)))
        remote(came, came, sent, mate_got.at[j], mate, rad).wait_recv()
        for t in range(bounds[j], bounds[j + 1]):
            step(t)

    for k in range(1, X):
        seg = source(k, c)
        remote(dens(seg), dens(seg), aux_sent, dens_got.at[k - 1], mate, rad).wait_recv()
        remote(dens(seg), dens(seg), aux_sent, mate_got.at[0], mate, rad).start()

    @pl.when(c == 1)
    def _():
        for j in range(K):
            take(j)

    for j in range(K):
        @pl.when(c == 0)
        def _():
            take(j, j < K - 1)

        finish(j)

    for count in range(3):
        @pl.when(neighbours == count)
        def _():
            gone = tiles(2 * ZR.shape[1] + (2 * X - 1) * T + (X - 1) * FX.shape[1] + count * 3 * T // R)
            remote(gone, gone, aux_sent, halo_got, mate, rad).wait_send()
    gone = tiles((2 * X - 1) * 3 * T)
    remote(gone, gone, sent, halo_got, mate, rad).wait_send()


def shards(fields, shifts, courant):
    n, rn = lax.axis_size("az"), lax.axis_size("rad")
    F, T, R, L = fields.shape
    X = n // 2
    bounds = sorted({T * b // BOUNDS[-1] for b in BOUNDS})
    K, fill = len(bounds) - 1, bounds[1]
    packs, fixes = -(-3 * T // L), -(-6 * fill // L)
    tile = R * L
    held = (n + 2) * F * T * tile + 3 * fill * tile + 2 * 3 * T * L + (4 * packs + n * fixes) * tile + 9 * T * tile
    grant = 4 * held + (2 << 20)
    dma = pltpu.SemaphoreType.DMA
    vmem = pl.BlockSpec(memory_space=pltpu.VMEM)
    return pl.pallas_call(
        functools.partial(kernel, n, rn, bounds),
        out_shape=jax.ShapeDtypeStruct(fields.shape, jnp.float32),
        in_specs=[pl.BlockSpec(memory_space=pltpu.HBM)] * 3,
        out_specs=vmem,
        scratch_shapes=[
            pltpu.VMEM((3, T, R, L), jnp.float32),
            pltpu.VMEM((3 * fill, R, L), jnp.float32),
            pltpu.VMEM((n * T, R, L), jnp.float32),
            pltpu.VMEM((n * T * 3, R, L), jnp.float32),
            pltpu.VMEM((2, 3, T, L), jnp.float32),
            pltpu.VMEM((2, packs, R, L), jnp.float32),
            pltpu.VMEM((2, packs, R, L), jnp.float32),
            pltpu.VMEM((n, fixes, R, L), jnp.float32),
            pltpu.VMEM((T, 4, R, L), jnp.int32),
            pltpu.VMEM((T, 4, R, L), jnp.int32),
            pltpu.VMEM((T, R, L), jnp.float32),
            pltpu.VMEM((R, T), jnp.int32),
            pltpu.VMEM((2, R, T), jnp.float32),
            dma(()), dma(()), dma(()), dma(()), dma(()), dma(()),
            dma((X - 1,)), dma((K, X - 1)), dma((K,)),
        ],
        compiler_params=pltpu.CompilerParams(collective_id=0, has_side_effects=True, vmem_limit_bytes=grant),
    )(*(pltpu.with_memory_space_constraint(v, pltpu.HBM) for v in (fields, shifts.T, courant.T)))


def solution(mesh):
    return jax.shard_map(
        shards,
        mesh=mesh,
        in_specs=(P(None, None, "rad", "az"), P(None, "rad"), P(None, "rad")),
        out_specs=P(None, None, "rad", "az"),
        check_vma=False,
    )
```

```python
import functools
import math

import jax
import jax.numpy as jnp
from jax import lax
from jax.experimental import pallas as pl
from jax.experimental.pallas import tpu as pltpu
from jax.sharding import PartitionSpec as P

inner_radius = 0.4
adiabatic = 1.4
MESH = pl.DeviceIdType.MESH
OFFSETS = (-2, -1, 0, 1)
BOUNDS = (0, 8, 11, 16)


def remote(src, dst, send, recv, az, rad):
    return pltpu.make_async_remote_copy(
        src_ref=src,
        dst_ref=dst,
        send_sem=send,
        recv_sem=recv,
        device_id={"az": az, "rad": rad},
        device_id_type=MESH,
    )


def minmod(a, b):
    return jnp.maximum(jnp.minimum(a, b), jnp.minimum(jnp.maximum(a, b), 0.0))


def kernel(n, rn, bounds, fields, shifts_in, courant_in, out, raw, early, D, G, H, ZS, ZR, FX, SEG, LANE, CA, shifts, courant,
           local_sem, small_sem, sent, aux_sent, halo_got, late_got, dens_got, got, mate_got):
    _, T, R, L = fields.shape
    X = n // 2
    K = len(bounds) - 1
    fill = bounds[1]
    az = lax.axis_index("az")
    rad = lax.axis_index("rad")
    x, c = az // 2, az % 2
    mate = x * 2 + (1 - c)
    before, after = lax.rem(az + n - 1, n), lax.rem(az + 1, n)

    def column(k, core=None):
        return lax.rem(x + k, X) * 2 + (c if core is None else core)

    def source(k, core):
        return lax.rem(x + X - k, X) * 2 + core

    def tiles(m):
        return G.at[pl.ds(0, m)]

    def dens(seg):
        return D.at[pl.ds(seg * T, T)]

    has_low, has_high = rad > 0, rad < rn - 1
    sends = (has_high, has_low)
    receives = (has_low, has_high)
    toward = (rad + 1, rad - 1)
    neighbours = has_low.astype(jnp.int32) + has_high.astype(jnp.int32)

    barrier = pltpu.get_barrier_semaphore()

    def greet(sem, a, r):
        pl.semaphore_signal(sem, inc=1, device_id={"az": a, "rad": r}, device_id_type=MESH)

    greet(barrier, mate, rad)
    for k in range(1, X):
        greet(barrier, column(k), rad)
        greet(barrier, column(k, 1 - c), rad)
    for way in range(2):
        @pl.when(sends[way])
        def _():
            greet(barrier, az, toward[way])

    small = (
        pltpu.make_async_copy(shifts_in, shifts, small_sem),
        pltpu.make_async_copy(courant_in, courant.at[0], small_sem),
    )
    local = (
        pltpu.make_async_copy(fields.at[0:3], raw, local_sem),
        pltpu.make_async_copy(fields.at[3], dens(az), local_sem),
    )
    for copy in small + local:
        copy.start()

    def density_out(from_ref):
        for k in range(1, X):
            remote(from_ref, dens(az), aux_sent, dens_got.at[k - 1], column(k), rad).start()

    parts = ((0, fill, halo_got), (fill, T - fill, late_got))

    def edge_copy(way, first, count, got_sem):
        some = pl.ds(first, count)
        return remote(raw.at[:, some, (R - 1) * (1 - way), :], H.at[way, :, some], aux_sent, got_sem, az, toward[way])

    def edges_out():
        for part in parts:
            for way in (1, 0):
                pl.when(sends[way])(edge_copy(way, *part).start)

    phi_count, rad_count = n * L, rn * R
    phi_step = 2.0 * math.pi / phi_count
    rad_step = 1.0 / rad_count
    spacing = min(rad_step, inner_radius * phi_step)
    dt = 0.2 * spacing
    viscosity = 0.05 * spacing * spacing / dt
    row = lax.broadcasted_iota(jnp.int32, (R, L), 0)
    lane = lax.broadcasted_iota(jnp.int32, (R, L), 1)
    radius = inner_radius + ((rad * R + row).astype(jnp.float32) + 0.5) * (1.0 / rad_count)
    width = radius * phi_step
    inv_r = 1.0 / radius
    inv_w = 1.0 / width
    spread_az = (dt * viscosity) * inv_w * inv_w
    spread_rad = dt * viscosity / (rad_step * rad_step)
    press_rad = dt * (adiabatic - 1.0) * 0.5 / rad_step
    press_az = (dt * (adiabatic - 1.0) * 0.5) * inv_w
    turn = dt * inv_r
    pull = dt * inv_r * inv_r
    heat = dt * (adiabatic - 1.0)
    heat_rad = heat * 0.5 / rad_step
    heat_az = (heat * 0.5) * inv_w
    heat_r = heat * inv_r
    bits = L.bit_length() - 1
    first_lane, last_lane = lane == 0, lane == L - 1
    first_row, last_row = row == 0, row == R - 1

    def turned(value, amount):
        return pltpu.roll(value, amount % L, 1) if amount % L else value

    pltpu.make_async_copy(tiles(4 * T), tiles(4 * T), local_sem).wait()

    for side in range(2):
        for p in range(ZS.shape[1]):
            packed = jnp.zeros((R, L), jnp.float32)
            for i in range(p * L, min(3 * T, (p + 1) * L)):
                packed = jnp.where(lane == i - p * L, turned(raw[i // T, i % T], i - p * L + side), packed)
            ZS[side, p] = packed

    for way in range(2):
        @pl.when(jnp.logical_not(receives[way]))
        def _():
            H[way] = raw[:, :, (R - 1) * way, :]

    def stencil(t, inner):
        vr, vp, en, den = raw[0, t], raw[1, t], raw[2, t], D[az * T + t]

        def around(f, q):
            i = f * T + t
            left, right = turned(q, 1), turned(q, L - 1)
            low, high = pltpu.roll(q, 1, 0), pltpu.roll(q, R - 1, 0)
            if not inner:
                left = jnp.where(first_lane, turned(ZR[0, i // L], -i), left)
                right = jnp.where(last_lane, turned(ZR[1, i // L], L - 1 - i), right)
                low = jnp.where(first_row, H[0, f, pl.ds(t, 1), :], low)
                high = jnp.where(last_row, H[1, f, pl.ds(t, 1), :], high)
            return left, right, low, high

        vl, vh, vd, vu = around(0, vr)
        pl_, ph, pd, pu = around(1, vp)
        el, eh, ed, eu = around(2, en)
        inv_den = 1.0 / den
        new_r = vr + (
            spread_az * (vh + vl - 2.0 * vr)
            + spread_rad * (vu + vd - 2.0 * vr)
            + (vp * vp * turn - pull)
            - press_rad * (eu - ed) * inv_den
        )
        new_p = vp + (
            spread_az * (ph + pl_ - 2.0 * vp)
            + spread_rad * (pu + pd - 2.0 * vp)
            - vr * vp * turn
            - press_az * (eh - el) * inv_den
        )
        new_e = en - en * (heat_rad * (vu - vd) + heat_az * (ph - pl_) + heat_r * vr)
        return new_r, new_p, new_e

    def place(seg, t):
        return (seg * T + t) * 3

    def block(seg, j):
        return G.at[pl.ds(place(seg, bounds[j]), 3 * (bounds[j + 1] - bounds[j]))]

    def side_copy(side):
        return remote(ZS.at[side], ZR.at[1 - side], aux_sent, halo_got, after if side else before, rad)

    pl.semaphore_wait(barrier, 2 * X - 1 + neighbours)

    edges_out()

    for side in range(2):
        side_copy(side).start()

    density_out(dens(az))

    for t in range(fill):
        for f, value in enumerate(stencil(t, True)):
            early[3 * t + f] = value
    for k in range(1, X):
        inside = pl.ds(1, R - 2)
        remote(early.at[:, inside], G.at[pl.ds(place(az, 0), 3 * fill), inside], sent, got.at[0, k - 1], column(k), rad).start()

    pltpu.make_async_copy(courant, courant, small_sem).wait()
    for t in range(T):
        moves = jnp.broadcast_to(shifts[:, t : t + 1], (R, L))
        cour = jnp.broadcast_to(courant[0, :, t : t + 1], (R, L))
        CA[t] = jnp.abs(cour)
        sign = jnp.where(cour >= 0.0, 1, -1)
        for o, offset in enumerate(OFFSETS):
            s = moves - sign * offset
            s = jnp.where(s < 0, s + phi_count, s)
            s = jnp.where(s >= phi_count, s - phi_count, s)
            q = s >> bits
            rest = s & (L - 1)
            seg = az - q - jnp.where(lane + rest >= L, 1, 0)
            SEG[t, o] = jnp.where(seg < 0, seg + n, seg)
            LANE[t, o] = (lane - rest) & (L - 1)

    for count in range(3):
        @pl.when(neighbours == count)
        def _():
            came = tiles(2 * ZR.shape[1] + count * 3 * fill // R)
            remote(came, came, aux_sent, halo_got, mate, rad).wait_recv()

    for j in range(K):
        if j == 1:
            for count in range(1, 3):
                @pl.when(neighbours == count)
                def _():
                    came = tiles(count * 3 * (T - fill) // R)
                    remote(came, came, aux_sent, late_got, mate, rad).wait_recv()

        for t in range(bounds[j], bounds[j + 1]):
            for f, value in enumerate(stencil(t, False)):
                G[place(az, t) + f] = value
        if j == 0:
            for k in range(1, X):
                for r in (0, R - 1):
                    line = G.at[pl.ds(place(az, 0), 3 * fill), r]
                    remote(line, line, sent, got.at[0, k - 1], column(k), rad).start()
            for p in range(FX.shape[1]):
                packed = jnp.zeros((R, L), jnp.float32)
                for i in range(p * L, min(6 * fill, (p + 1) * L)):
                    packed = jnp.where(lane == i - p * L, turned(G[place(az, 0) + i // 2], i - p * L + i % 2), packed)
                FX[az, p] = packed
            for k in range(1, X):
                remote(FX.at[az], FX.at[az], aux_sent, got.at[0, k - 1], column(k), rad).start()
        else:
            for k in range(1, X):
                remote(block(az, j), block(az, j), sent, got.at[j, k - 1], column(k), rad).start()
                if j == K - 1:
                    direct = remote(block(az, j), block(az, j), sent, mate_got.at[j], column(k, 1), rad)
                    pl.when(c == 0)(direct.start)
    remote(dens(az), dens(az), aux_sent, mate_got.at[0], mate, rad).start()
    for j in range(K):
        remote(block(az, j), block(az, j), sent, mate_got.at[j], mate, rad).start()

    def step(t):
        amount = CA[t]
        half = 0.5 * (1.0 - amount)
        taken = [[] for _ in range(4)]
        moved = [[G[place(s, t) + f] for f in range(3)] + [D[s * T + t]] for s in range(n)]
        for o in range(len(OFFSETS)):
            seg, at = SEG[t, o], LANE[t, o]
            chosen = [seg == s for s in range(n - 1)]
            for f in range(4):
                value = moved[n - 1][f]
                for s in range(n - 1):
                    value = jnp.where(chosen[s], moved[s][f], value)
                taken[f].append(jnp.take_along_axis(value, at, axis=1, mode="promise_in_bounds"))
        for f in range(4):
            q0, q1, q2, q3 = taken[f]
            d0, d1, d2 = q1 - q0, q2 - q1, q3 - q2
            enters = q1 + half * minmod(d0, d1)
            leaves = q2 + half * minmod(d1, d2)
            out[f, t] = q2 - amount * (leaves - enters)

    def take(j, forward=True):
        for k in range(1, X):
            seg = source(k, c)
            came = tiles(3 * (bounds[j + 1] - bounds[j]) + (0 if j else FX.shape[1]))
            remote(came, came, sent, got.at[j, k - 1], mate, rad).wait_recv()
            if j == 0:
                for i in range(3 * fill):
                    p, at = 2 * i // L, 2 * i % L
                    value = jnp.where(first_lane, turned(FX[seg, p], -at), G[place(seg, 0) + i])
                    G[place(seg, 0) + i] = jnp.where(last_lane, turned(FX[seg, p], L - 2 - at), value)
            if forward:
                remote(block(seg, j), block(seg, j), sent, mate_got.at[j], mate, rad).start()

    def arrive(j):
        came = tiles(X * (3 * (bounds[j + 1] - bounds[j]) + (0 if j else T)))
        remote(came, came, sent, mate_got.at[j], mate, rad).wait_recv()

    for k in range(1, X):
        seg = source(k, c)
        remote(dens(seg), dens(seg), aux_sent, dens_got.at[k - 1], mate, rad).wait_recv()
        remote(dens(seg), dens(seg), aux_sent, mate_got.at[0], mate, rad).start()

    @pl.when(c == 1)
    def _():
        for j in range(K):
            take(j)

    for group in [(j,) for j in range(K - 2)] + [(K - 2, K - 1)]:
        @pl.when(c == 0)
        def _():
            for j in group:
                take(j, j < K - 1)

        for j in group:
            arrive(j)
        for t in range(bounds[group[0]], bounds[group[-1] + 1]):
            step(t)

    for count in range(3):
        @pl.when(neighbours == count)
        def _():
            gone = tiles(2 * ZR.shape[1] + (2 * X - 1) * T + (X - 1) * FX.shape[1] + count * 3 * T // R)
            remote(gone, gone, aux_sent, halo_got, mate, rad).wait_send()
    gone = tiles((2 * X - 1) * 3 * T)
    remote(gone, gone, sent, halo_got, mate, rad).wait_send()


def shards(fields, shifts, courant):
    n, rn = lax.axis_size("az"), lax.axis_size("rad")
    F, T, R, L = fields.shape
    X = n // 2
    bounds = sorted({T * b // BOUNDS[-1] for b in BOUNDS})
    K, fill = len(bounds) - 1, bounds[1]
    packs, fixes = -(-3 * T // L), -(-6 * fill // L)
    tile = R * L
    held = (n + 2) * F * T * tile + 3 * fill * tile + 2 * 3 * T * L + (4 * packs + n * fixes) * tile + 9 * T * tile
    grant = 4 * held + (2 << 20)
    dma = pltpu.SemaphoreType.DMA
    vmem = pl.BlockSpec(memory_space=pltpu.VMEM)
    return pl.pallas_call(
        functools.partial(kernel, n, rn, bounds),
        out_shape=jax.ShapeDtypeStruct(fields.shape, jnp.float32),
        in_specs=[pl.BlockSpec(memory_space=pltpu.HBM)] * 3,
        out_specs=vmem,
        scratch_shapes=[
            pltpu.VMEM((3, T, R, L), jnp.float32),
            pltpu.VMEM((3 * fill, R, L), jnp.float32),
            pltpu.VMEM((n * T, R, L), jnp.float32),
            pltpu.VMEM((n * T * 3, R, L), jnp.float32),
            pltpu.VMEM((2, 3, T, L), jnp.float32),
            pltpu.VMEM((2, packs, R, L), jnp.float32),
            pltpu.VMEM((2, packs, R, L), jnp.float32),
            pltpu.VMEM((n, fixes, R, L), jnp.float32),
            pltpu.VMEM((T, 4, R, L), jnp.int32),
            pltpu.VMEM((T, 4, R, L), jnp.int32),
            pltpu.VMEM((T, R, L), jnp.float32),
            pltpu.VMEM((R, T), jnp.int32),
            pltpu.VMEM((2, R, T), jnp.float32),
            dma(()), dma(()), dma(()), dma(()), dma(()), dma(()),
            dma((X - 1,)), dma((K, X - 1)), dma((K,)),
        ],
        compiler_params=pltpu.CompilerParams(collective_id=0, has_side_effects=True, vmem_limit_bytes=grant),
    )(*(pltpu.with_memory_space_constraint(v, pltpu.HBM) for v in (fields, shifts.T, courant.T)))


def solution(mesh):
    return jax.shard_map(
        shards,
        mesh=mesh,
        in_specs=(P(None, None, "rad", "az"), P(None, "rad"), P(None, "rad")),
        out_specs=P(None, None, "rad", "az"),
        check_vma=False,
    )
```

```python
import functools
import math

import jax
import jax.numpy as jnp
from jax import lax
from jax.experimental import pallas as pl
from jax.experimental.pallas import tpu as pltpu
from jax.sharding import PartitionSpec as P

inner_radius = 0.4
adiabatic = 1.4
MESH = pl.DeviceIdType.MESH
OFFSETS = (-2, -1, 0, 1)
BOUNDS = (0, 8, 11, 16)


def remote(src, dst, send, recv, az, rad):
    return pltpu.make_async_remote_copy(
        src_ref=src,
        dst_ref=dst,
        send_sem=send,
        recv_sem=recv,
        device_id={"az": az, "rad": rad},
        device_id_type=MESH,
    )


def minmod(a, b):
    return jnp.maximum(jnp.minimum(a, b), jnp.minimum(jnp.maximum(a, b), 0.0))


def kernel(n, rn, bounds, fields, shifts_in, courant_in, out, raw, early, D, G, H, ZS, ZR, FX, SEG, LANE, CA, shifts, courant,
           local_sem, small_sem, sent, aux_sent, halo_got, late_got, dens_got, got, mate_got):
    _, T, R, L = fields.shape
    X = n // 2
    K = len(bounds) - 1
    fill = bounds[1]
    az = lax.axis_index("az")
    rad = lax.axis_index("rad")
    x, c = az // 2, az % 2
    mate = x * 2 + (1 - c)
    before, after = lax.rem(az + n - 1, n), lax.rem(az + 1, n)

    def column(k, core=None):
        return lax.rem(x + k, X) * 2 + (c if core is None else core)

    def source(k, core):
        return lax.rem(x + X - k, X) * 2 + core

    def tiles(m):
        return G.at[pl.ds(0, m)]

    def dens(seg):
        return D.at[pl.ds(seg * T, T)]

    has_low, has_high = rad > 0, rad < rn - 1
    sends = (has_high, has_low)
    receives = (has_low, has_high)
    toward = (rad + 1, rad - 1)
    neighbours = has_low.astype(jnp.int32) + has_high.astype(jnp.int32)

    barrier = pltpu.get_barrier_semaphore()

    def greet(sem, a, r):
        pl.semaphore_signal(sem, inc=1, device_id={"az": a, "rad": r}, device_id_type=MESH)

    greet(barrier, mate, rad)
    for k in range(1, X):
        greet(barrier, column(k), rad)
        greet(barrier, column(k, 1 - c), rad)
    for way in range(2):
        @pl.when(sends[way])
        def _():
            greet(barrier, az, toward[way])

    small = (
        pltpu.make_async_copy(shifts_in, shifts, small_sem),
        pltpu.make_async_copy(courant_in, courant.at[0], small_sem),
    )
    local = (
        pltpu.make_async_copy(fields.at[0:3], raw, local_sem),
        pltpu.make_async_copy(fields.at[3], dens(az), local_sem),
    )
    for copy in small + local:
        copy.start()

    def density_out(from_ref):
        for k in range(1, X):
            remote(from_ref, dens(az), aux_sent, dens_got.at[k - 1], column(k), rad).start()

    parts = ((0, fill, halo_got), (fill, T - fill, late_got))

    def edge_copy(way, first, count, got_sem):
        some = pl.ds(first, count)
        return remote(raw.at[:, some, (R - 1) * (1 - way), :], H.at[way, :, some], aux_sent, got_sem, az, toward[way])

    def edges_out():
        for part in parts:
            for way in (1, 0):
                pl.when(sends[way])(edge_copy(way, *part).start)

    phi_count, rad_count = n * L, rn * R
    phi_step = 2.0 * math.pi / phi_count
    rad_step = 1.0 / rad_count
    spacing = min(rad_step, inner_radius * phi_step)
    dt = 0.2 * spacing
    viscosity = 0.05 * spacing * spacing / dt
    row = lax.broadcasted_iota(jnp.int32, (R, L), 0)
    lane = lax.broadcasted_iota(jnp.int32, (R, L), 1)
    radius = inner_radius + ((rad * R + row).astype(jnp.float32) + 0.5) * (1.0 / rad_count)
    width = radius * phi_step
    inv_r = 1.0 / radius
    inv_w = 1.0 / width
    spread_az = (dt * viscosity) * inv_w * inv_w
    spread_rad = dt * viscosity / (rad_step * rad_step)
    press_rad = dt * (adiabatic - 1.0) * 0.5 / rad_step
    press_az = (dt * (adiabatic - 1.0) * 0.5) * inv_w
    turn = dt * inv_r
    pull = dt * inv_r * inv_r
    heat = dt * (adiabatic - 1.0)
    heat_rad = heat * 0.5 / rad_step
    heat_az = (heat * 0.5) * inv_w
    heat_r = heat * inv_r
    bits = L.bit_length() - 1
    first_lane, last_lane = lane == 0, lane == L - 1
    first_row, last_row = row == 0, row == R - 1

    def turned(value, amount):
        return pltpu.roll(value, amount % L, 1) if amount % L else value

    pltpu.make_async_copy(tiles(4 * T), tiles(4 * T), local_sem).wait()

    for side in range(2):
        for p in range(ZS.shape[1]):
            packed = jnp.zeros((R, L), jnp.float32)
            for i in range(p * L, min(3 * T, (p + 1) * L)):
                packed = jnp.where(lane == i - p * L, turned(raw[i // T, i % T], i - p * L + side), packed)
            ZS[side, p] = packed

    for way in range(2):
        @pl.when(jnp.logical_not(receives[way]))
        def _():
            H[way] = raw[:, :, (R - 1) * way, :]

    def stencil(t, inner):
        vr, vp, en, den = raw[0, t], raw[1, t], raw[2, t], D[az * T + t]

        def around(f, q):
            i = f * T + t
            left, right = turned(q, 1), turned(q, L - 1)
            low, high = pltpu.roll(q, 1, 0), pltpu.roll(q, R - 1, 0)
            if not inner:
                left = jnp.where(first_lane, turned(ZR[0, i // L], -i), left)
                right = jnp.where(last_lane, turned(ZR[1, i // L], L - 1 - i), right)
                low = jnp.where(first_row, H[0, f, pl.ds(t, 1), :], low)
                high = jnp.where(last_row, H[1, f, pl.ds(t, 1), :], high)
            return left, right, low, high

        vl, vh, vd, vu = around(0, vr)
        pl_, ph, pd, pu = around(1, vp)
        el, eh, ed, eu = around(2, en)
        inv_den = 1.0 / den
        new_r = vr + (
            spread_az * (vh + vl - 2.0 * vr)
            + spread_rad * (vu + vd - 2.0 * vr)
            + (vp * vp * turn - pull)
            - press_rad * (eu - ed) * inv_den
        )
        new_p = vp + (
            spread_az * (ph + pl_ - 2.0 * vp)
            + spread_rad * (pu + pd - 2.0 * vp)
            - vr * vp * turn
            - press_az * (eh - el) * inv_den
        )
        new_e = en - en * (heat_rad * (vu - vd) + heat_az * (ph - pl_) + heat_r * vr)
        return new_r, new_p, new_e

    def place(seg, t):
        return (seg * T + t) * 3

    def block(seg, j):
        return G.at[pl.ds(place(seg, bounds[j]), 3 * (bounds[j + 1] - bounds[j]))]

    def side_copy(side):
        return remote(ZS.at[side], ZR.at[1 - side], aux_sent, halo_got, after if side else before, rad)

    pl.semaphore_wait(barrier, 2 * X - 1 + neighbours)

    edges_out()

    for side in range(2):
        side_copy(side).start()

    density_out(dens(az))

    for t in range(fill):
        for f, value in enumerate(stencil(t, True)):
            early[3 * t + f] = value
    for k in range(1, X):
        inside = pl.ds(1, R - 2)
        remote(early.at[:, inside], G.at[pl.ds(place(az, 0), 3 * fill), inside], sent, got.at[0, k - 1], column(k), rad).start()

    pltpu.make_async_copy(courant, courant, small_sem).wait()
    for t in range(T):
        moves = jnp.broadcast_to(shifts[:, t : t + 1], (R, L))
        cour = jnp.broadcast_to(courant[0, :, t : t + 1], (R, L))
        CA[t] = jnp.abs(cour)
        sign = jnp.where(cour >= 0.0, 1, -1)
        for o, offset in enumerate(OFFSETS):
            s = moves - sign * offset
            s = jnp.where(s < 0, s + phi_count, s)
            s = jnp.where(s >= phi_count, s - phi_count, s)
            q = s >> bits
            rest = s & (L - 1)
            seg = az - q - jnp.where(lane + rest >= L, 1, 0)
            SEG[t, o] = jnp.where(seg < 0, seg + n, seg)
            LANE[t, o] = (lane - rest) & (L - 1)

    for count in range(3):
        @pl.when(neighbours == count)
        def _():
            came = tiles(2 * ZR.shape[1] + count * 3 * fill // R)
            remote(came, came, aux_sent, halo_got, mate, rad).wait_recv()

    for j in range(K):
        if j == 1:
            for count in range(1, 3):
                @pl.when(neighbours == count)
                def _():
                    came = tiles(count * 3 * (T - fill) // R)
                    remote(came, came, aux_sent, late_got, mate, rad).wait_recv()

        for t in range(bounds[j], bounds[j + 1]):
            for f, value in enumerate(stencil(t, False)):
                G[place(az, t) + f] = value
        if j == 0:
            for k in range(1, X):
                for r in (0, R - 1):
                    line = G.at[pl.ds(place(az, 0), 3 * fill), r]
                    remote(line, line, sent, got.at[0, k - 1], column(k), rad).start()
            for p in range(FX.shape[1]):
                packed = jnp.zeros((R, L), jnp.float32)
                for i in range(p * L // 2, min(3 * fill, (p + 1) * L // 2)):
                    at = 2 * i - p * L
                    packed = jnp.where(lane >> 1 == at // 2, turned(G[place(az, 0) + i], at + 1), packed)
                FX[az, p] = packed
            for k in range(1, X):
                remote(FX.at[az], FX.at[az], aux_sent, got.at[0, k - 1], column(k), rad).start()
        else:
            for k in range(1, X):
                remote(block(az, j), block(az, j), sent, got.at[j, k - 1], column(k), rad).start()
                if j == K - 1:
                    direct = remote(block(az, j), block(az, j), sent, mate_got.at[j], column(k, 1), rad)
                    pl.when(c == 0)(direct.start)
    remote(dens(az), dens(az), aux_sent, mate_got.at[0], mate, rad).start()
    for j in range(K):
        remote(block(az, j), block(az, j), sent, mate_got.at[j], mate, rad).start()

    def step(t):
        amount = CA[t]
        half = 0.5 * (1.0 - amount)
        taken = [[] for _ in range(4)]
        moved = [[G[place(s, t) + f] for f in range(3)] + [D[s * T + t]] for s in range(n)]
        for o in range(len(OFFSETS)):
            seg, at = SEG[t, o], LANE[t, o]
            chosen = [seg == s for s in range(n - 1)]
            for f in range(4):
                value = moved[n - 1][f]
                for s in range(n - 1):
                    value = jnp.where(chosen[s], moved[s][f], value)
                taken[f].append(jnp.take_along_axis(value, at, axis=1, mode="promise_in_bounds"))
        for f in range(4):
            q0, q1, q2, q3 = taken[f]
            d0, d1, d2 = q1 - q0, q2 - q1, q3 - q2
            enters = q1 + half * minmod(d0, d1)
            leaves = q2 + half * minmod(d1, d2)
            out[f, t] = q2 - amount * (leaves - enters)

    def take(j, forward=True):
        for k in range(1, X):
            seg = source(k, c)
            came = tiles(3 * (bounds[j + 1] - bounds[j]) + (0 if j else FX.shape[1]))
            remote(came, came, sent, got.at[j, k - 1], mate, rad).wait_recv()
            if j == 0:
                for i in range(3 * fill):
                    p, at = 2 * i // L, 2 * i % L
                    G[place(seg, 0) + i] = jnp.where(first_lane | last_lane, turned(FX[seg, p], -at - 1), G[place(seg, 0) + i])
            if forward:
                remote(block(seg, j), block(seg, j), sent, mate_got.at[j], mate, rad).start()

    def arrive(j):
        came = tiles(X * (3 * (bounds[j + 1] - bounds[j]) + (0 if j else T)))
        remote(came, came, sent, mate_got.at[j], mate, rad).wait_recv()

    for k in range(1, X):
        seg = source(k, c)
        remote(dens(seg), dens(seg), aux_sent, dens_got.at[k - 1], mate, rad).wait_recv()
        remote(dens(seg), dens(seg), aux_sent, mate_got.at[0], mate, rad).start()

    @pl.when(c == 1)
    def _():
        for j in range(K):
            take(j)

    for group in [(j,) for j in range(K - 2)] + [(K - 2, K - 1)]:
        @pl.when(c == 0)
        def _():
            for j in group:
                take(j, j < K - 1)

        for j in group:
            arrive(j)
        for t in range(bounds[group[0]], bounds[group[-1] + 1]):
            step(t)

    for count in range(3):
        @pl.when(neighbours == count)
        def _():
            gone = tiles(2 * ZR.shape[1] + (2 * X - 1) * T + (X - 1) * FX.shape[1] + count * 3 * T // R)
            remote(gone, gone, aux_sent, halo_got, mate, rad).wait_send()
    gone = tiles((2 * X - 1) * 3 * T)
    remote(gone, gone, sent, halo_got, mate, rad).wait_send()


def shards(fields, shifts, courant):
    n, rn = lax.axis_size("az"), lax.axis_size("rad")
    F, T, R, L = fields.shape
    X = n // 2
    bounds = sorted({T * b // BOUNDS[-1] for b in BOUNDS})
    K, fill = len(bounds) - 1, bounds[1]
    packs, fixes = -(-3 * T // L), -(-6 * fill // L)
    tile = R * L
    held = (n + 2) * F * T * tile + 3 * fill * tile + 2 * 3 * T * L + (4 * packs + n * fixes) * tile + 9 * T * tile
    grant = 4 * held + (2 << 20)
    dma = pltpu.SemaphoreType.DMA
    vmem = pl.BlockSpec(memory_space=pltpu.VMEM)
    return pl.pallas_call(
        functools.partial(kernel, n, rn, bounds),
        out_shape=jax.ShapeDtypeStruct(fields.shape, jnp.float32),
        in_specs=[pl.BlockSpec(memory_space=pltpu.HBM)] * 3,
        out_specs=vmem,
        scratch_shapes=[
            pltpu.VMEM((3, T, R, L), jnp.float32),
            pltpu.VMEM((3 * fill, R, L), jnp.float32),
            pltpu.VMEM((n * T, R, L), jnp.float32),
            pltpu.VMEM((n * T * 3, R, L), jnp.float32),
            pltpu.VMEM((2, 3, T, L), jnp.float32),
            pltpu.VMEM((2, packs, R, L), jnp.float32),
            pltpu.VMEM((2, packs, R, L), jnp.float32),
            pltpu.VMEM((n, fixes, R, L), jnp.float32),
            pltpu.VMEM((T, 4, R, L), jnp.int32),
            pltpu.VMEM((T, 4, R, L), jnp.int32),
            pltpu.VMEM((T, R, L), jnp.float32),
            pltpu.VMEM((R, T), jnp.int32),
            pltpu.VMEM((2, R, T), jnp.float32),
            dma(()), dma(()), dma(()), dma(()), dma(()), dma(()),
            dma((X - 1,)), dma((K, X - 1)), dma((K,)),
        ],
        compiler_params=pltpu.CompilerParams(collective_id=0, has_side_effects=True, vmem_limit_bytes=grant),
    )(*(pltpu.with_memory_space_constraint(v, pltpu.HBM) for v in (fields, shifts.T, courant.T)))


def solution(mesh):
    return jax.shard_map(
        shards,
        mesh=mesh,
        in_specs=(P(None, None, "rad", "az"), P(None, "rad"), P(None, "rad")),
        out_specs=P(None, None, "rad", "az"),
        check_vma=False,
    )
```

```python
import functools
import math

import jax
import jax.numpy as jnp
from jax import lax
from jax.experimental import pallas as pl
from jax.experimental.pallas import tpu as pltpu
from jax.sharding import PartitionSpec as P

inner_radius = 0.4
adiabatic = 1.4
MESH = pl.DeviceIdType.MESH
OFFSETS = (-2, -1, 0, 1)
BOUNDS = (0, 8, 10, 16)


def remote(src, dst, send, recv, az, rad):
    return pltpu.make_async_remote_copy(
        src_ref=src,
        dst_ref=dst,
        send_sem=send,
        recv_sem=recv,
        device_id={"az": az, "rad": rad},
        device_id_type=MESH,
    )


def minmod(a, b):
    return jnp.maximum(jnp.minimum(a, b), jnp.minimum(jnp.maximum(a, b), 0.0))


def kernel(n, rn, bounds, fields, shifts_in, courant_in, out, raw, early, D, G, H, ZS, ZR, FX, SEG, LANE, CA, shifts, courant,
           local_sem, small_sem, sent, aux_sent, halo_got, late_got, dens_got, got, mate_got):
    _, T, R, L = fields.shape
    X = n // 2
    K = len(bounds) - 1
    fill = bounds[1]
    az = lax.axis_index("az")
    rad = lax.axis_index("rad")
    x, c = az // 2, az % 2
    mate = x * 2 + (1 - c)
    before, after = lax.rem(az + n - 1, n), lax.rem(az + 1, n)

    def column(k, core=None):
        return lax.rem(x + k, X) * 2 + (c if core is None else core)

    def source(k, core):
        return lax.rem(x + X - k, X) * 2 + core

    def tiles(m):
        return G.at[pl.ds(0, m)]

    def dens(seg):
        return D.at[pl.ds(seg * T, T)]

    has_low, has_high = rad > 0, rad < rn - 1
    sends = (has_high, has_low)
    receives = (has_low, has_high)
    toward = (rad + 1, rad - 1)
    neighbours = has_low.astype(jnp.int32) + has_high.astype(jnp.int32)

    barrier = pltpu.get_barrier_semaphore()

    def greet(sem, a, r):
        pl.semaphore_signal(sem, inc=1, device_id={"az": a, "rad": r}, device_id_type=MESH)

    greet(barrier, mate, rad)
    for k in range(1, X):
        greet(barrier, column(k), rad)
        greet(barrier, column(k, 1 - c), rad)
    for way in range(2):
        @pl.when(sends[way])
        def _():
            greet(barrier, az, toward[way])

    small = (
        pltpu.make_async_copy(shifts_in, shifts, small_sem),
        pltpu.make_async_copy(courant_in, courant.at[0], small_sem),
    )
    local = (
        pltpu.make_async_copy(fields.at[0:3], raw, local_sem),
        pltpu.make_async_copy(fields.at[3], dens(az), local_sem),
    )
    for copy in small + local:
        copy.start()

    def density_out(from_ref):
        for k in range(1, X):
            remote(from_ref, dens(az), aux_sent, dens_got.at[k - 1], column(k), rad).start()

    parts = ((0, fill, halo_got), (fill, T - fill, late_got))

    def edge_copy(way, first, count, got_sem):
        some = pl.ds(first, count)
        return remote(raw.at[:, some, (R - 1) * (1 - way), :], H.at[way, :, some], aux_sent, got_sem, az, toward[way])

    def edges_out():
        for part in parts:
            for way in (1, 0):
                pl.when(sends[way])(edge_copy(way, *part).start)

    phi_count, rad_count = n * L, rn * R
    phi_step = 2.0 * math.pi / phi_count
    rad_step = 1.0 / rad_count
    spacing = min(rad_step, inner_radius * phi_step)
    dt = 0.2 * spacing
    viscosity = 0.05 * spacing * spacing / dt
    row = lax.broadcasted_iota(jnp.int32, (R, L), 0)
    lane = lax.broadcasted_iota(jnp.int32, (R, L), 1)
    radius = inner_radius + ((rad * R + row).astype(jnp.float32) + 0.5) * (1.0 / rad_count)
    width = radius * phi_step
    inv_r = 1.0 / radius
    inv_w = 1.0 / width
    spread_az = (dt * viscosity) * inv_w * inv_w
    spread_rad = dt * viscosity / (rad_step * rad_step)
    press_rad = dt * (adiabatic - 1.0) * 0.5 / rad_step
    press_az = (dt * (adiabatic - 1.0) * 0.5) * inv_w
    turn = dt * inv_r
    pull = dt * inv_r * inv_r
    heat = dt * (adiabatic - 1.0)
    heat_rad = heat * 0.5 / rad_step
    heat_az = (heat * 0.5) * inv_w
    heat_r = heat * inv_r
    bits = L.bit_length() - 1
    first_lane, last_lane = lane == 0, lane == L - 1
    first_row, last_row = row == 0, row == R - 1

    def turned(value, amount):
        return pltpu.roll(value, amount % L, 1) if amount % L else value

    pltpu.make_async_copy(tiles(4 * T), tiles(4 * T), local_sem).wait()

    for side in range(2):
        for p in range(ZS.shape[1]):
            packed = jnp.zeros((R, L), jnp.float32)
            for i in range(p * L, min(3 * T, (p + 1) * L)):
                packed = jnp.where(lane == i - p * L, turned(raw[i // T, i % T], i - p * L + side), packed)
            ZS[side, p] = packed

    for way in range(2):
        @pl.when(jnp.logical_not(receives[way]))
        def _():
            H[way] = raw[:, :, (R - 1) * way, :]

    def stencil(t, inner):
        vr, vp, en, den = raw[0, t], raw[1, t], raw[2, t], D[az * T + t]

        def around(f, q):
            i = f * T + t
            left, right = turned(q, 1), turned(q, L - 1)
            low, high = pltpu.roll(q, 1, 0), pltpu.roll(q, R - 1, 0)
            if not inner:
                left = jnp.where(first_lane, turned(ZR[0, i // L], -i), left)
                right = jnp.where(last_lane, turned(ZR[1, i // L], L - 1 - i), right)
                low = jnp.where(first_row, H[0, f, pl.ds(t, 1), :], low)
                high = jnp.where(last_row, H[1, f, pl.ds(t, 1), :], high)
            return left, right, low, high

        vl, vh, vd, vu = around(0, vr)
        pl_, ph, pd, pu = around(1, vp)
        el, eh, ed, eu = around(2, en)
        inv_den = 1.0 / den
        new_r = vr + (
            spread_az * (vh + vl - 2.0 * vr)
            + spread_rad * (vu + vd - 2.0 * vr)
            + (vp * vp * turn - pull)
            - press_rad * (eu - ed) * inv_den
        )
        new_p = vp + (
            spread_az * (ph + pl_ - 2.0 * vp)
            + spread_rad * (pu + pd - 2.0 * vp)
            - vr * vp * turn
            - press_az * (eh - el) * inv_den
        )
        new_e = en - en * (heat_rad * (vu - vd) + heat_az * (ph - pl_) + heat_r * vr)
        return new_r, new_p, new_e

    def place(seg, t):
        return (seg * T + t) * 3

    def block(seg, j):
        return G.at[pl.ds(place(seg, bounds[j]), 3 * (bounds[j + 1] - bounds[j]))]

    def side_copy(side):
        return remote(ZS.at[side], ZR.at[1 - side], aux_sent, halo_got, after if side else before, rad)

    pl.semaphore_wait(barrier, 2 * X - 1 + neighbours)

    edges_out()

    for side in range(2):
        side_copy(side).start()

    density_out(dens(az))

    for t in range(fill):
        for f, value in enumerate(stencil(t, True)):
            early[3 * t + f] = value
    for k in range(1, X):
        inside = pl.ds(1, R - 2)
        remote(early.at[:, inside], G.at[pl.ds(place(az, 0), 3 * fill), inside], sent, got.at[0, k - 1], column(k), rad).start()

    pltpu.make_async_copy(courant, courant, small_sem).wait()
    for t in range(T):
        moves = jnp.broadcast_to(shifts[:, t : t + 1], (R, L))
        cour = jnp.broadcast_to(courant[0, :, t : t + 1], (R, L))
        CA[t] = jnp.abs(cour)
        sign = jnp.where(cour >= 0.0, 1, -1)
        for o, offset in enumerate(OFFSETS):
            s = moves - sign * offset
            s = jnp.where(s < 0, s + phi_count, s)
            s = jnp.where(s >= phi_count, s - phi_count, s)
            q = s >> bits
            rest = s & (L - 1)
            seg = az - q - jnp.where(lane + rest >= L, 1, 0)
            SEG[t, o] = jnp.where(seg < 0, seg + n, seg)
            LANE[t, o] = (lane - rest) & (L - 1)

    for count in range(3):
        @pl.when(neighbours == count)
        def _():
            came = tiles(2 * ZR.shape[1] + count * 3 * fill // R)
            remote(came, came, aux_sent, halo_got, mate, rad).wait_recv()

    for j in range(K):
        if j == 1:
            for count in range(1, 3):
                @pl.when(neighbours == count)
                def _():
                    came = tiles(count * 3 * (T - fill) // R)
                    remote(came, came, aux_sent, late_got, mate, rad).wait_recv()

        for t in range(bounds[j], bounds[j + 1]):
            for f, value in enumerate(stencil(t, False)):
                G[place(az, t) + f] = value
        if j == 0:
            for k in range(1, X):
                for r in (0, R - 1):
                    line = G.at[pl.ds(place(az, 0), 3 * fill), r]
                    remote(line, line, sent, got.at[0, k - 1], column(k), rad).start()
            for p in range(FX.shape[1]):
                packed = jnp.zeros((R, L), jnp.float32)
                for i in range(p * L // 2, min(3 * fill, (p + 1) * L // 2)):
                    at = 2 * i - p * L
                    packed = jnp.where(lane >> 1 == at // 2, turned(G[place(az, 0) + i], at + 1), packed)
                FX[az, p] = packed
            for k in range(1, X):
                remote(FX.at[az], FX.at[az], aux_sent, got.at[0, k - 1], column(k), rad).start()
        else:
            for k in range(1, X):
                remote(block(az, j), block(az, j), sent, got.at[j, k - 1], column(k), rad).start()
                if j == K - 1:
                    direct = remote(block(az, j), block(az, j), sent, mate_got.at[j], column(k, 1), rad)
                    pl.when(c == 0)(direct.start)
    remote(dens(az), dens(az), aux_sent, mate_got.at[0], mate, rad).start()
    for j in range(K):
        remote(block(az, j), block(az, j), sent, mate_got.at[j], mate, rad).start()

    def step(t):
        amount = CA[t]
        half = 0.5 * (1.0 - amount)
        taken = [[] for _ in range(4)]
        moved = [[G[place(s, t) + f] for f in range(3)] + [D[s * T + t]] for s in range(n)]
        for o in range(len(OFFSETS)):
            seg, at = SEG[t, o], LANE[t, o]
            chosen = [seg == s for s in range(n - 1)]
            for f in range(4):
                value = moved[n - 1][f]
                for s in range(n - 1):
                    value = jnp.where(chosen[s], moved[s][f], value)
                taken[f].append(jnp.take_along_axis(value, at, axis=1, mode="promise_in_bounds"))
        for f in range(4):
            q0, q1, q2, q3 = taken[f]
            d0, d1, d2 = q1 - q0, q2 - q1, q3 - q2
            enters = q1 + half * minmod(d0, d1)
            leaves = q2 + half * minmod(d1, d2)
            out[f, t] = q2 - amount * (leaves - enters)

    def take(j, forward=True):
        for k in range(1, X):
            seg = source(k, c)
            came = tiles(3 * (bounds[j + 1] - bounds[j]) + (0 if j else FX.shape[1]))
            remote(came, came, sent, got.at[j, k - 1], mate, rad).wait_recv()
            if j == 0:
                for i in range(3 * fill):
                    p, at = 2 * i // L, 2 * i % L
                    G[place(seg, 0) + i] = jnp.where(first_lane | last_lane, turned(FX[seg, p], -at - 1), G[place(seg, 0) + i])
            if forward:
                remote(block(seg, j), block(seg, j), sent, mate_got.at[j], mate, rad).start()

    def arrive(j):
        came = tiles(X * (3 * (bounds[j + 1] - bounds[j]) + (0 if j else T)))
        remote(came, came, sent, mate_got.at[j], mate, rad).wait_recv()

    for k in range(1, X):
        seg = source(k, c)
        remote(dens(seg), dens(seg), aux_sent, dens_got.at[k - 1], mate, rad).wait_recv()
        remote(dens(seg), dens(seg), aux_sent, mate_got.at[0], mate, rad).start()

    @pl.when(c == 1)
    def _():
        for j in range(K):
            take(j)

    for group in [(j,) for j in range(K - 2)] + [(K - 2, K - 1)]:
        @pl.when(c == 0)
        def _():
            for j in group:
                take(j, j < K - 1)

        for j in group:
            arrive(j)
        for t in range(bounds[group[0]], bounds[group[-1] + 1]):
            step(t)

    for count in range(3):
        @pl.when(neighbours == count)
        def _():
            gone = tiles(2 * ZR.shape[1] + (2 * X - 1) * T + (X - 1) * FX.shape[1] + count * 3 * T // R)
            remote(gone, gone, aux_sent, halo_got, mate, rad).wait_send()
    gone = tiles((2 * X - 1) * 3 * T)
    remote(gone, gone, sent, halo_got, mate, rad).wait_send()


def shards(fields, shifts, courant):
    n, rn = lax.axis_size("az"), lax.axis_size("rad")
    F, T, R, L = fields.shape
    X = n // 2
    bounds = sorted({T * b // BOUNDS[-1] for b in BOUNDS})
    K, fill = len(bounds) - 1, bounds[1]
    packs, fixes = -(-3 * T // L), -(-6 * fill // L)
    tile = R * L
    held = (n + 2) * F * T * tile + 3 * fill * tile + 2 * 3 * T * L + (4 * packs + n * fixes) * tile + 9 * T * tile
    grant = 4 * held + (2 << 20)
    dma = pltpu.SemaphoreType.DMA
    vmem = pl.BlockSpec(memory_space=pltpu.VMEM)
    return pl.pallas_call(
        functools.partial(kernel, n, rn, bounds),
        out_shape=jax.ShapeDtypeStruct(fields.shape, jnp.float32),
        in_specs=[pl.BlockSpec(memory_space=pltpu.HBM)] * 3,
        out_specs=vmem,
        scratch_shapes=[
            pltpu.VMEM((3, T, R, L), jnp.float32),
            pltpu.VMEM((3 * fill, R, L), jnp.float32),
            pltpu.VMEM((n * T, R, L), jnp.float32),
            pltpu.VMEM((n * T * 3, R, L), jnp.float32),
            pltpu.VMEM((2, 3, T, L), jnp.float32),
            pltpu.VMEM((2, packs, R, L), jnp.float32),
            pltpu.VMEM((2, packs, R, L), jnp.float32),
            pltpu.VMEM((n, fixes, R, L), jnp.float32),
            pltpu.VMEM((T, 4, R, L), jnp.int32),
            pltpu.VMEM((T, 4, R, L), jnp.int32),
            pltpu.VMEM((T, R, L), jnp.float32),
            pltpu.VMEM((R, T), jnp.int32),
            pltpu.VMEM((2, R, T), jnp.float32),
            dma(()), dma(()), dma(()), dma(()), dma(()), dma(()),
            dma((X - 1,)), dma((K, X - 1)), dma((K,)),
        ],
        compiler_params=pltpu.CompilerParams(collective_id=0, has_side_effects=True, vmem_limit_bytes=grant),
    )(*(pltpu.with_memory_space_constraint(v, pltpu.HBM) for v in (fields, shifts.T, courant.T)))


def solution(mesh):
    return jax.shard_map(
        shards,
        mesh=mesh,
        in_specs=(P(None, None, "rad", "az"), P(None, "rad"), P(None, "rad")),
        out_specs=P(None, None, "rad", "az"),
        check_vma=False,
    )
```
